32 devices in a mesh: dp: 8 (over y, x, core), mp: 4 (over z).
Axes of the slice: x: 2, y: 2, z: 4, core: 2. Of those that a mesh axis runs over, the one named last changes fastest.
Arguments:
- tokens: bfloat16 [2048, 8192], P('dp', 'mp'), may hold values from -8 to 8
- attn_gain: bfloat16 [8192], replicated, may hold values from 0.5 to 1.5
- w_query: bfloat16 [8192, 4096], P('dp', 'mp'), may hold values from -2 to 2
- key_projection_weight: bfloat16 [8192, 512], P('dp', 'mp'), may hold values from -2 to 2
- value_projection_weight: bfloat16 [8192, 512], P('dp', 'mp'), may hold values from -0.0625 to 0.0625
- w_out: bfloat16 [4096, 8192], P('mp', 'dp'), may hold values from -0.09375 to 0.09375
- final_gain: bfloat16 [8192], P('mp'), may hold values from 0.5 to 1.5
- unembed: bfloat16 [64128, 8192], P('dp', 'mp'), may hold values from -0.29882812 to 0.29882812
- clean_ids: int32 [8], replicated, may hold values from 0 to 64127, as said below
- corrupt_ids: int32 [8], replicated, may hold values from 0 to 64127
Outputs:
- head_out: bfloat16 [2048, 4096], P('dp', 'mp')
- scores: float32 [8, 32], P('dp', 'mp')
- metric: float32 [8], P('dp')
The draws below stay inside these ranges and needn't reach their ends.
Inputs may be any that keep to these rules, and one draw needn't show every extreme that they name: `clean_ids`: split the ids into 8 aligned blocks of equal size and number the groups of 1 sequence alike; the block of a clean answer, minus the number of its sequence's group, taken modulo the number of blocks, is drawn so that every such offset occurs for some sequence.
All inputs are finite; a program needn't handle non-finite values.
Results may differ from the reference program's by a relative error of at most 0.015.
Values may be sent and summed in bfloat16 or wider, within the bound.
A program may use at most 128 MiB of HBM per device.

```python
import math
import jax
import jax.numpy as jnp
from jax import lax

MODEL_WIDTH = 8192
QUERY_HEADS = 32
KEY_VALUE_HEADS = 4
HEAD_SIZE = 128
VOCAB = 64128
SEQUENCE_LENGTH = 256
SEQ_DEV = 1
SEQS = 8
TOKENS = 2048


def draw_tokens(key, part):
    key_common, key_jitter, key_shared = jax.random.split(jax.random.fold_in(key, 7), 3)
    common = jax.random.normal(key_common, (1, 1, MODEL_WIDTH), jnp.float32)
    ramp_up = jnp.arange(SEQS, dtype=jnp.float32) / max(SEQS - 1, 1)
    jitter = jax.random.uniform(key_jitter, (SEQS,), jnp.float32, 0.7, 1.3)
    perturbation_scale = 0.3 * 10.0 ** ramp_up * jitter
    random_perturbation = jax.random.normal(key_shared, (SEQS, SEQUENCE_LENGTH, MODEL_WIDTH), jnp.float32)
    drawn = random_perturbation + perturbation_scale[:, None, None] * common
    return jnp.clip(drawn, -8.0, 8.0).reshape(TOKENS, MODEL_WIDTH).astype(jnp.bfloat16)


def paired_weights(key):
    random_key_for_key = jax.random.fold_in(jax.random.fold_in(key, 23), 0)
    key_query = jax.random.fold_in(jax.random.fold_in(key, 23), 3)
    key_matrix = jax.random.normal(random_key_for_key, (MODEL_WIDTH, KEY_VALUE_HEADS * HEAD_SIZE), jnp.float32) / math.sqrt(MODEL_WIDTH)
    query_matrix = jax.random.normal(key_query, (MODEL_WIDTH, QUERY_HEADS * HEAD_SIZE), jnp.float32) / math.sqrt(MODEL_WIDTH)
    return (jnp.clip(query_matrix, -2.0, 2.0), jnp.clip(key_matrix, -2.0, 2.0))


def draw_w_query(key, part):
    return paired_weights(key)[0].astype(jnp.bfloat16)


def draw_key_projection_weight(key, part):
    return paired_weights(key)[1].astype(jnp.bfloat16)


def draw_clean_ids(key, part):
    key_order, key_inner = jax.random.split(jax.random.fold_in(key, 41), 2)
    group_count = SEQS // SEQ_DEV
    block_size = VOCAB // group_count
    shuffled = jax.random.permutation(key_order, group_count).astype(jnp.int32)
    offsets = (shuffled - shuffled[0] + group_count - 1) % group_count
    seq_index = jnp.arange(SEQS, dtype=jnp.int32)
    owner = seq_index // SEQ_DEV
    block = (owner + offsets[seq_index % group_count]) % group_count
    inner = jax.random.randint(key_inner, (SEQS,), 0, block_size, jnp.int32)
    inner = jnp.where(seq_index == 0, block_size - 1, inner)
    return (block * block_size + inner).astype(jnp.int32)


def set_ends(values, key, smallest, top_value):
    dims = values.shape
    spot = [jax.random.randint(jax.random.fold_in(key, axis), (), 0, dims[axis]) for axis in range(len(dims))]
    values = values.at[tuple(spot)].set(smallest)
    longest = dims.index(max(dims))
    spot[longest] = (spot[longest] + 1) % dims[longest]
    return values.at[tuple(spot)].set(top_value)


def level_of(rng, dims, shards, low, top_value):
    def one(axis_at, parts):
        heights = jax.random.uniform(jax.random.fold_in(jax.random.fold_in(rng, 6), axis_at), (parts,), jnp.float32, low / len(shards), top_value / len(shards))
        return jnp.repeat(jnp.exp(heights), dims[axis_at] // parts).reshape((-1,) + (1,) * (len(dims) - axis_at - 1))

    loudness = one(*shards[0])
    for cut in shards[1:]:
        loudness = loudness * one(*cut)
    return loudness


def normal_values(stream_key, extent, width, bound, pieces=(), kind=jnp.bfloat16):
    factor_of = level_of(stream_key, extent, pieces, -0.22, 0.18) if pieces else 1.0
    values = jax.random.normal(stream_key, extent, jnp.float32) * width * factor_of
    return jnp.minimum(jnp.maximum(values, -bound), bound).astype(kind)


def setup_inputs(seed: int = 0) -> dict:
    arg_keys = jax.random.split(jax.random.key(seed), 11)
    tokens = draw_tokens(jax.random.fold_in(arg_keys[10], 71), 0)
    attn_gain = jnp.clip(1.0 + 0.1 * jax.random.normal(arg_keys[1], (MODEL_WIDTH,), jnp.float32), 0.5, 1.5).astype(jnp.bfloat16)
    w_query = draw_w_query(jax.random.fold_in(arg_keys[10], 71), 0)
    key_projection_weight = draw_key_projection_weight(jax.random.fold_in(arg_keys[10], 71), 0)
    value_projection_weight = normal_values(arg_keys[4], (MODEL_WIDTH, KEY_VALUE_HEADS * HEAD_SIZE), MODEL_WIDTH ** -0.5, 0.0625, ((0, 8), (1, 4)))
    w_out = normal_values(arg_keys[5], (QUERY_HEADS * HEAD_SIZE, MODEL_WIDTH), (QUERY_HEADS * HEAD_SIZE) ** -0.5, 0.09375, ((0, 4), (1, 8)))
    final_gain = jnp.clip(1.0 + 0.1 * jax.random.normal(arg_keys[6], (MODEL_WIDTH,), jnp.float32), 0.5, 1.5).astype(jnp.bfloat16)
    unembed = normal_values(arg_keys[7], (VOCAB, MODEL_WIDTH), 0.05, 0.29882812, ((0, 8), (1, 4)))
    clean_ids = draw_clean_ids(jax.random.fold_in(arg_keys[10], 71), 0)
    corrupt_ids = set_ends(jax.random.randint(arg_keys[9], (SEQS,), 0, VOCAB), jax.random.fold_in(arg_keys[9], 1), 0, VOCAB - 1).astype(jnp.int32)
    return dict(tokens=tokens, attn_gain=attn_gain, w_query=w_query, key_projection_weight=key_projection_weight, value_projection_weight=value_projection_weight, w_out=w_out, final_gain=final_gain, unembed=unembed, clean_ids=clean_ids, corrupt_ids=corrupt_ids)


def apply_rotary(tensor, length):
    half_dim = tensor.shape[-1] // 2
    positions = jnp.arange(length, dtype=jnp.float32)
    inv_freq = jnp.exp(jnp.arange(half_dim, dtype=jnp.float32) * (-2.0 * math.log(500000.0) / tensor.shape[-1]))
    angles = positions[:, None] * inv_freq[None, :]
    cosine_table = jnp.cos(angles)[:, None, :]
    sine_table = jnp.sin(angles)[:, None, :]
    lower_half = tensor[..., :half_dim]
    upper_half = tensor[..., half_dim:]
    return jnp.concatenate([lower_half * cosine_table - upper_half * sine_table, upper_half * cosine_table + lower_half * sine_table], axis=-1)

def attend(queries, projected_key_rows, value_rows):
    length, q_heads, head_dim = queries.shape
    kv_heads = projected_key_rows.shape[1]
    grouped = queries.reshape(length, kv_heads, q_heads // kv_heads, head_dim)
    logits = jnp.einsum('tkgd,skd->kgts', grouped.astype(jnp.float32), projected_key_rows.astype(jnp.float32)) / math.sqrt(head_dim)
    causal = jnp.arange(length)[:, None] >= jnp.arange(length)[None, :]
    logits = jnp.where(causal, logits, -1e+30)
    row_top = lax.optimization_barrier(jnp.max(logits, axis=-1, keepdims=True))
    exponent = jnp.exp(logits - row_top)
    attn_probs = (exponent / lax.optimization_barrier(jnp.sum(exponent, axis=-1, keepdims=True))).astype(jnp.bfloat16)
    mixed_heads = jnp.einsum('kgts,skd->tkgd', attn_probs.astype(jnp.float32), value_rows.astype(jnp.float32))
    return mixed_heads.astype(jnp.bfloat16).reshape(length, q_heads * head_dim)

def reference(tokens, attn_gain, w_query, key_projection_weight, value_projection_weight, w_out, final_gain, unembed, clean_ids, corrupt_ids):

    def one_sequence(tokens_seq):
        wide = tokens_seq.astype(jnp.float32)
        normalized_rows = (wide * lax.rsqrt(lax.optimization_barrier(jnp.mean(wide * wide, axis=1, keepdims=True)) + 1e-05) * attn_gain.astype(jnp.float32)).astype(jnp.bfloat16)
        queries = apply_rotary(jnp.dot(normalized_rows, w_query, preferred_element_type=jnp.float32).reshape(SEQUENCE_LENGTH, QUERY_HEADS, HEAD_SIZE), SEQUENCE_LENGTH).astype(jnp.bfloat16)
        projected_key_rows = apply_rotary(jnp.dot(normalized_rows, key_projection_weight, preferred_element_type=jnp.float32).reshape(SEQUENCE_LENGTH, KEY_VALUE_HEADS, HEAD_SIZE), SEQUENCE_LENGTH).astype(jnp.bfloat16)
        value_rows = jnp.dot(normalized_rows, value_projection_weight, preferred_element_type=jnp.float32).astype(jnp.bfloat16).reshape(SEQUENCE_LENGTH, KEY_VALUE_HEADS, HEAD_SIZE)
        return attend(queries, projected_key_rows, value_rows)
    per_seq = lax.map(one_sequence, tokens.reshape(SEQS, SEQUENCE_LENGTH, MODEL_WIDTH))
    head_out = per_seq.reshape(TOKENS, QUERY_HEADS * HEAD_SIZE)
    head_mean = lax.optimization_barrier(jnp.sum(head_out.astype(jnp.float32), axis=0)) / TOKENS
    last_out = per_seq[:, SEQUENCE_LENGTH - 1, :]
    attn_last = jnp.dot(last_out, w_out, preferred_element_type=jnp.float32).astype(jnp.bfloat16)
    residual = tokens.reshape(SEQS, SEQUENCE_LENGTH, MODEL_WIDTH)[:, SEQUENCE_LENGTH - 1, :].astype(jnp.float32) + attn_last.astype(jnp.float32)
    direction = unembed[clean_ids].astype(jnp.float32) - unembed[corrupt_ids].astype(jnp.float32)
    weighted = final_gain.astype(jnp.float32) * direction
    inverse = lax.rsqrt(lax.optimization_barrier(jnp.mean(residual * residual, axis=1)) + 1e-05)
    metric = inverse * lax.optimization_barrier(jnp.sum(residual * weighted, axis=1))
    grad_last = (weighted * inverse[:, None] - residual * (metric * inverse * inverse / MODEL_WIDTH)[:, None]).astype(jnp.bfloat16)
    head_grads = jnp.dot(grad_last, w_out.T, preferred_element_type=jnp.float32)
    mean_gap = head_mean[None, :] - last_out.astype(jnp.float32)
    scores = lax.optimization_barrier(jnp.sum((mean_gap * head_grads).reshape(SEQS, QUERY_HEADS, HEAD_SIZE), axis=2))
    return (head_out, scores, metric)
```

```python
import functools
import math

import jax
import jax.numpy as jnp
from jax import lax
from jax.experimental import pallas as pl
from jax.experimental.pallas import tpu as pltpu
from jax.sharding import PartitionSpec as P

HEAD_SIZE = 128
SEQUENCE_LENGTH = 256
MESH = pl.DeviceIdType.MESH
F32 = jnp.float32
BF16 = jnp.bfloat16


def flip(index, mask):
    bit = 1
    out = index
    while bit <= mask:
        if mask & bit:
            out = out + bit - 2 * bit * ((index // bit) % 2)
        bit *= 2
    return out


def spread_plan(size):
    bits = []
    bit = 2
    while bit < size:
        bits.append(bit)
        bit *= 2
    parts = min(2, len(bits))
    plan = []
    for part in range(parts):
        order = bits[part:] + bits[:part]
        held = [0]
        arrivals = []
        for step, b in enumerate(order):
            fresh = [h ^ b for h in held]
            arrivals += [(f, step) for f in fresh]
            held = held + fresh
        plan.append((order, arrivals))
    return plan


def project_kernel(
    D, M, chunks, xchunks,
    tok_ref, gain_ref, wq_ref, wk_ref, wv_ref, out_ref,
    x_all, w_all, loc_sem, xloc_sem, xs_sem, xr_sem, ps_sem, pr_sem, cs_sem, cr_sem,
):
    d = lax.axis_index("dp")
    m = lax.axis_index("mp")
    plan = spread_plan(D)
    parts = len(plan)
    n_bits = D.bit_length() - 1
    depth = wq_ref.shape[0]
    rows = tok_ref.shape[0]
    width = tok_ref.shape[1]
    qw, kw, vw = wq_ref.shape[1], wk_ref.shape[1], wv_ref.shape[1]
    piece = depth // (parts * chunks)
    xpiece = rows // xchunks

    def wrows(p, c):
        return pl.ds((p * chunks + c) * piece, piece)

    own = []
    for c in range(chunks):
        for p in range(parts):
            rr = wrows(p, c)
            trio = []
            for i, (src, lo, n) in enumerate(
                ((wq_ref, 0, qw), (wk_ref, qw, kw), (wv_ref, qw + kw, vw))
            ):
                cp = pltpu.make_async_copy(
                    src.at[rr, :], w_all.at[d, rr, pl.ds(lo, n)], loc_sem.at[p, c, i]
                )
                cp.start()
                trio.append(cp)
            own.append((p, c, trio))
    xown = pltpu.make_async_copy(tok_ref, x_all.at[m], xloc_sem)
    xown.start()

    barrier = pltpu.get_barrier_semaphore()
    for b in range(n_bits):
        pl.semaphore_signal(barrier, inc=1, device_id=(flip(d, 1 << b), m), device_id_type=MESH)

    @pl.when(m > 0)
    def _():
        pl.semaphore_signal(barrier, inc=1, device_id=(d, m - 1), device_id_type=MESH)

    @pl.when(m < M - 1)
    def _():
        pl.semaphore_signal(barrier, inc=1, device_id=(d, m + 1), device_id_type=MESH)

    pl.semaphore_wait(barrier, n_bits + jnp.where(m > 0, 1, 0) + jnp.where(m < M - 1, 1, 0))

    def xsend(hop, c, side):
        rr = pl.ds(c * xpiece, xpiece)
        owner = m - hop if side == 0 else m + hop
        to = m + 1 if side == 0 else m - 1
        return pltpu.make_async_remote_copy(
            src_ref=(tok_ref.at[rr, :] if hop == 0 else x_all.at[owner, rr, :]),
            dst_ref=x_all.at[owner, rr, :],
            send_sem=xs_sem.at[hop, c, side],
            recv_sem=xr_sem.at[hop, c, side],
            device_id=(d, to),
            device_id_type=MESH,
        )

    def xpred(hop, side):
        if side == 0:
            return (m < M - 1) & (m - hop >= 0)
        return (m > 0) & (m + hop < M)

    def xstart(hop, c):
        for side in range(2):
            @pl.when(xpred(hop, side))
            def _(side=side):
                xsend(hop, c, side).start()

    def xwait(hop, c):
        rr = pl.ds(c * xpiece, xpiece)
        for side in range(2):
            owner = m - hop - 1 if side == 0 else m + hop + 1
            ok = (m - hop - 1 >= 0) if side == 0 else (m + hop + 1 < M)

            @pl.when(ok)
            def _(side=side, owner=owner):
                pltpu.make_async_copy(
                    x_all.at[owner, rr, :], x_all.at[owner, rr, :], xr_sem.at[hop, c, side]
                ).wait()

    for c in range(xchunks):
        xstart(0, c)

    sends = []

    def wcopy(mask, p, c, bit, send_sem, recv_sem):
        owner = flip(d, mask)
        rr = wrows(p, c)
        return pltpu.make_async_remote_copy(
            src_ref=w_all.at[owner, rr, :],
            dst_ref=w_all.at[owner, rr, :],
            send_sem=send_sem,
            recv_sem=recv_sem,
            device_id=(flip(d, bit), m),
            device_id_type=MESH,
        )

    def wsend(mask, p, c, step):
        bit = plan[p][0][step]
        cp = wcopy(mask, p, c, bit, ps_sem.at[p, mask // 2, c, step],
                   pr_sem.at[p, (mask ^ bit) // 2, c])
        cp.start()
        sends.append(cp)

    def csend(mask, p, c):
        cp = wcopy(mask, p, c, 1, cs_sem.at[p, mask // 2, c], cr_sem.at[p, mask // 2, c])
        cp.start()
        sends.append(cp)

    def wwait(mask, p, c, sem):
        owner = flip(d, mask)
        rr = wrows(p, c)
        pltpu.make_async_copy(w_all.at[owner, rr, :], w_all.at[owner, rr, :], sem).wait()

    steps = len(plan[0][0])
    for p, c, trio in own:
        for cp in trio:
            cp.wait()
        wsend(0, p, c, 0)
    for step in range(1, steps):
        for c in range(chunks):
            for p in range(parts):
                wsend(0, p, c, step)
    for c in range(chunks):
        for p in range(parts):
            csend(0, p, c)

    rounds = len(plan[0][1])
    wevents = [(r, c) for r in range(rounds) for c in range(chunks)]
    xevents = [(h, c) for h in range(M - 1) for c in range(xchunks)]
    merged = sorted(
        [((i + 1) / len(wevents), 1, e) for i, e in enumerate(wevents)]
        + [(0.8 * (i + 1) / len(xevents), 0, e) for i, e in enumerate(xevents)]
    )

    def take(r, c):
        for p in range(parts):
            mask, step = plan[p][1][r]
            wwait(mask, p, c, pr_sem.at[p, mask // 2, c])
            for later in range(step + 1, steps):
                wsend(mask, p, c, later)
            csend(mask, p, c)

    def use(owner, lo, n):
        base = owner * depth
        shard = base // width
        col = pl.multiple_of(base % width + lo, 128 if n % 128 == 0 else n)
        out_ref[...] += jnp.dot(
            x_all[shard, :, pl.ds(col, n)], w_all[owner, pl.ds(lo, n), :],
            preferred_element_type=F32,
        )

    x_left = len(xevents)
    for _, kind, (a, c) in merged:
        if kind == 0:
            xwait(a, c)
            if a + 1 < M - 1:
                xstart(a + 1, c)
            x_left -= 1
            if x_left == 0:
                xown.wait()
                total = jnp.zeros((rows, 1), F32)
                for k in range(M):
                    xv = x_all[k].astype(F32)
                    total = total + jnp.sum(xv * xv, axis=1, keepdims=True)
                inv = lax.rsqrt(total / (M * width) + 1e-05)
                for h in range(M - 1):
                    for cc in range(xchunks):
                        for side in range(2):
                            @pl.when(xpred(h, side))
                            def _(h=h, cc=cc, side=side):
                                xsend(h, cc, side).wait_send()
                for k in range(M):
                    g = gain_ref[:, k * width:(k + 1) * width].astype(F32)
                    x_all[k] = (x_all[k].astype(F32) * inv * g).astype(BF16)
                out_ref[...] = jnp.zeros_like(out_ref)
        else:
            take(a, c)
    order = [0]
    for r in range(rounds):
        for p in range(parts):
            if plan[p][1][r][0] not in order:
                order.append(plan[p][1][r][0])
    for mask in order:
        use(flip(d, mask), 0, depth)
    for mask in order:
        for p in range(parts):
            for c in range(chunks):
                wwait(mask + 1, p, c, cr_sem.at[p, mask // 2, c])
        use(flip(d, mask + 1), 0, depth)
    for cp in sends:
        cp.wait_send()


def project(D, M, tokens, gain, wq, wk, wv):
    rows, width = tokens.shape
    depth = wq.shape[0]
    total = wq.shape[1] + wk.shape[1] + wv.shape[1]
    parts = len(spread_plan(D))
    steps = len(spread_plan(D)[0][0])
    chunks = 2 if depth // (2 * parts) >= 128 else 1
    xchunks = 2
    half = D // 2
    DMA = pltpu.SemaphoreType.DMA
    ANY = pl.BlockSpec(memory_space=pl.ANY)
    return pl.pallas_call(
        functools.partial(project_kernel, D, M, chunks, xchunks),
        name="project",
        out_shape=jax.ShapeDtypeStruct((rows, total), F32),
        in_specs=[ANY, pl.BlockSpec(memory_space=pltpu.VMEM), ANY, ANY, ANY],
        out_specs=pl.BlockSpec(memory_space=pltpu.VMEM),
        scratch_shapes=[
            pltpu.VMEM((M, rows, width), BF16),
            pltpu.VMEM((D, depth, total), BF16),
            DMA((parts, chunks, 3)),
            DMA(()),
            DMA((M - 1, xchunks, 2)),
            DMA((M - 1, xchunks, 2)),
            DMA((parts, half, chunks, steps)),
            DMA((parts, half, chunks)),
            DMA((parts, half, chunks)),
            DMA((parts, half, chunks)),
        ],
        compiler_params=pltpu.CompilerParams(
            collective_id=0, has_side_effects=True, vmem_limit_bytes=56 * 1024 * 1024
        ),
    )(tokens, gain, wq, wk, wv)


def attend_kernel(q_ref, k_ref, v_ref, cos_ref, sin_ref, out_ref, stat_ref):
    cos, sin = cos_ref[...], sin_ref[...]
    half = HEAD_SIZE // 2

    def rope(x):
        turned = jnp.concatenate([x[:, half:], x[:, :half]], axis=1)
        return (x * cos + turned * sin).astype(BF16)

    q, k = rope(q_ref[...]), rope(k_ref[...])
    v = v_ref[...].astype(BF16)
    length = q.shape[0]
    logits = lax.dot_general(
        q, k, (((1,), (1,)), ((), ())), preferred_element_type=F32
    ) / math.sqrt(HEAD_SIZE)
    at = lax.broadcasted_iota(jnp.int32, (length, length), 0)
    key_at = lax.broadcasted_iota(jnp.int32, (length, length), 1)
    logits = jnp.where(at >= key_at, logits, -1e30)
    top = jnp.max(logits, axis=1, keepdims=True)
    e = jnp.exp(logits - top)
    probs = (e / jnp.sum(e, axis=1, keepdims=True)).astype(BF16)
    mixed = jnp.dot(probs, v, preferred_element_type=F32).astype(BF16)
    out_ref[...] = mixed
    wide = mixed.astype(F32)
    stat_ref[0:1, :] = jnp.sum(wide, axis=0, keepdims=True)
    stat_ref[1:2, :] = wide[length - 1:length, :]


def attend(qkv, q_heads, kv_heads):
    rows = qkv.shape[0]
    S = rows // SEQUENCE_LENGTH
    group = q_heads // kv_heads
    half = HEAD_SIZE // 2
    inv_freq = jnp.exp(jnp.arange(half, dtype=F32) * (-2.0 * math.log(500000.0) / HEAD_SIZE))
    angles = jnp.arange(SEQUENCE_LENGTH, dtype=F32)[:, None] * inv_freq[None, :]
    c, s = jnp.cos(angles), jnp.sin(angles)
    cos = jnp.concatenate([c, c], axis=1)
    sin = jnp.concatenate([-s, s], axis=1)
    block = (SEQUENCE_LENGTH, HEAD_SIZE)
    table = pl.BlockSpec(block, lambda b, h: (0, 0))
    return pl.pallas_call(
        attend_kernel,
        name="attend",
        grid=(S, q_heads),
        in_specs=[
            pl.BlockSpec(block, lambda b, h: (b, h)),
            pl.BlockSpec(block, lambda b, h: (b, q_heads + h // group)),
            pl.BlockSpec(block, lambda b, h: (b, q_heads + kv_heads + h // group)),
            table,
            table,
        ],
        out_specs=[
            pl.BlockSpec(block, lambda b, h: (b, h)),
            pl.BlockSpec((None, 2, HEAD_SIZE), lambda b, h: (b, 0, h)),
        ],
        out_shape=[
            jax.ShapeDtypeStruct((rows, q_heads * HEAD_SIZE), BF16),
            jax.ShapeDtypeStruct((S, 2, q_heads * HEAD_SIZE), F32),
        ],
    )(qkv, qkv, qkv, cos, sin)


def tail_kernel(
    D, M, S, heads, token_count, model_width,
    stat_ref, wout_ref, contrib_ref, tok_ref, gain_ref, scores_ref, metric_ref,
    stat_all, rows_a, out_src, out_all, dir_all, sq_src, sq_all, g_src, g_all, hg_src, hg_all,
    s1, r1, s2, r2, s3, r3, s5, r5, s6, r6, s7, r7,
):
    d = lax.axis_index("dp")
    m = lax.axis_index("mp")
    R = D // M
    cols = wout_ref.shape[1]
    everyone = D * M
    me = d * M + m

    barrier = pltpu.get_barrier_semaphore()

    @pl.loop(1, everyone)
    def _(i):
        other = (me + i) % everyone
        pl.semaphore_signal(
            barrier, inc=1, device_id=(other // M, other % M), device_id_type=MESH
        )

    pl.semaphore_wait(barrier, everyone - 1)

    pending = []

    def remote(src, dst, ss, rs, to, cond=None):
        cp = pltpu.make_async_remote_copy(
            src_ref=src, dst_ref=dst, send_sem=ss, recv_sem=rs, device_id=to, device_id_type=MESH
        )
        if cond is None:
            cp.start()
        else:
            pl.when(cond)(cp.start)
        pending.append((cp, cond))

    def local(src, dst, rs, cond=None):
        cp = pltpu.make_async_copy(src, dst, rs)
        if cond is None:
            cp.start()
        else:
            pl.when(cond)(cp.start)

    def arrive(buf, sem, n):
        for i in range(n):
            pltpu.make_async_copy(buf.at[i], buf.at[i], sem.at[i]).wait()

    for i in range(1, D):
        to = (d + i) % D
        remote(stat_ref, stat_all.at[d], s1.at[i], r1.at[d], (to, m))
    local(stat_ref, stat_all.at[d], r1.at[d])
    for i in range(1, D):
        to = (d + i) % D
        remote(contrib_ref.at[to], dir_all.at[d], s2.at[i], r2.at[d], (to, m))
    local(contrib_ref.at[d], dir_all.at[d], r2.at[d])

    arrive(stat_all, r1, D)
    for j in range(D):
        for b in range(S):
            rows_a[j * S + b:j * S + b + 1, :] = stat_all[j, 2 * b + 1:2 * b + 2, :]
    w = wout_ref[...]
    partial = jnp.dot(rows_a[...].astype(BF16), w, preferred_element_type=F32)
    for j in range(D):
        out_src[j] = partial[j * S:(j + 1) * S, :]
    span = d // R
    slot = (d % R) * M + m
    for i in range(D):
        to = (d + i) % D
        if i == 0:
            remote(out_src.at[to], out_all.at[slot], s3.at[i], r3.at[slot], (to, span), m != span)
            local(out_src.at[to], out_all.at[slot], r3.at[slot], m == span)
        else:
            remote(out_src.at[to], out_all.at[slot], s3.at[i], r3.at[slot], (to, span))

    mean = jnp.zeros((1, stat_all.shape[2]), F32)
    for j in range(D):
        for b in range(S):
            mean = mean + stat_all[j, 2 * b:2 * b + 1, :]
    mean = mean / token_count
    arrive(dir_all, r2, D)
    direction = dir_all[0]
    for j in range(1, D):
        direction = direction + dir_all[j]
    weighted = gain_ref[...].astype(F32) * direction

    arrive(out_all, r3, D)
    pieces = []
    for jj in range(R):
        acc = out_all[jj * M]
        for k in range(1, M):
            acc = acc + out_all[jj * M + k]
        pieces.append(acc)
    attn_last = jnp.concatenate(pieces, axis=1).astype(BF16).astype(F32)
    residual = tok_ref[...].astype(F32) + attn_last
    sq_src[0] = jnp.broadcast_to(jnp.sum(residual * residual, axis=1, keepdims=True), (S, 128))
    sq_src[1] = jnp.broadcast_to(jnp.sum(residual * weighted, axis=1, keepdims=True), (S, 128))
    for i in range(1, M):
        to = (m + i) % M
        remote(sq_src, sq_all.at[m], s5.at[i], r5.at[m], (d, to))
    local(sq_src, sq_all.at[m], r5.at[m])
    arrive(sq_all, r5, M)
    square = sq_all[0, 0]
    product = sq_all[0, 1]
    for k in range(1, M):
        square = square + sq_all[k, 0]
        product = product + sq_all[k, 1]
    inverse = lax.rsqrt(square / model_width + 1e-05)
    metric = inverse * product
    metric_ref[...] = metric[:, 0:1]
    grad = weighted * inverse[:, 0:1] - residual * (
        metric * inverse * inverse / model_width
    )[:, 0:1]
    for jj in range(R):
        g_src[jj] = grad[:, jj * cols:(jj + 1) * cols].astype(BF16).astype(F32)
    for jj in range(R):
        to = m * R + jj
        for i in range(M):
            k = (m + i) % M
            if i == 0:
                remote(g_src.at[jj], g_all.at[d], s6.at[jj, i], r6.at[d], (to, k), to != d)
                local(g_src.at[jj], g_all.at[d], r6.at[d], to == d)
            else:
                remote(g_src.at[jj], g_all.at[d], s6.at[jj, i], r6.at[d], (to, k))
    arrive(g_all, r6, D)
    for j in range(D):
        rows_a[j * S:(j + 1) * S, 0:cols] = g_all[j]
    hg = lax.dot_general(
        rows_a[:, 0:cols].astype(BF16), w, (((1,), (1,)), ((), ())), preferred_element_type=F32
    )
    for j in range(D):
        hg_src[j] = hg[j * S:(j + 1) * S, :]
    for i in range(1, D):
        to = (d + i) % D
        remote(hg_src.at[to], hg_all.at[d], s7.at[i], r7.at[d], (to, m))
    local(hg_src.at[d], hg_all.at[d], r7.at[d])
    arrive(hg_all, r7, D)
    grads = hg_all[0]
    for j in range(1, D):
        grads = grads + hg_all[j]
    lasts = [stat_ref[2 * b + 1:2 * b + 2, :] for b in range(S)]
    last = lasts[0] if S == 1 else jnp.concatenate(lasts, axis=0)
    gap = (mean - last) * grads
    lane = lax.broadcasted_iota(jnp.int32, (S, heads), 1)
    scores = jnp.zeros((S, heads), F32)
    for h in range(heads):
        part = jnp.sum(gap[:, h * HEAD_SIZE:(h + 1) * HEAD_SIZE], axis=1, keepdims=True)
        scores = jnp.where(lane == h, part, scores)
    scores_ref[...] = scores
    for cp, cond in pending:
        if cond is None:
            cp.wait_send()
        else:
            pl.when(cond)(cp.wait_send)


def tail(D, M, stat, w_out, contrib, last_tokens, final_gain, token_count):
    S = stat.shape[0]
    entries, cols = w_out.shape
    width = last_tokens.shape[1]
    heads = entries // HEAD_SIZE
    R = D // M
    DMA = pltpu.SemaphoreType.DMA
    V = pl.BlockSpec(memory_space=pltpu.VMEM)
    wide = max(entries, cols)
    return pl.pallas_call(
        functools.partial(tail_kernel, D, M, S, heads, token_count, cols * D),
        name="tail",
        out_shape=[jax.ShapeDtypeStruct((S, heads), F32), jax.ShapeDtypeStruct((S, 1), F32)],
        in_specs=[V] * 5,
        out_specs=[V, V],
        scratch_shapes=[
            pltpu.VMEM((D, 2 * S, entries), F32),
            pltpu.VMEM((D * S, wide), F32),
            pltpu.VMEM((D, S, cols), F32),
            pltpu.VMEM((D, S, cols), F32),
            pltpu.VMEM((D, S, width), F32),
            pltpu.VMEM((2, S, 128), F32),
            pltpu.VMEM((M, 2, S, 128), F32),
            pltpu.VMEM((R, S, cols), F32),
            pltpu.VMEM((D, S, cols), F32),
            pltpu.VMEM((D, S, entries), F32),
            pltpu.VMEM((D, S, entries), F32),
            DMA((D,)), DMA((D,)), DMA((D,)), DMA((D,)), DMA((D,)), DMA((D,)),
            DMA((M,)), DMA((M,)), DMA((R, M)), DMA((D,)), DMA((D,)), DMA((D,)),
        ],
        compiler_params=pltpu.CompilerParams(
            collective_id=1, has_side_effects=True, vmem_limit_bytes=32 * 1024 * 1024
        ),
    )(stat.reshape(2 * S, entries), w_out, contrib, last_tokens, final_gain.reshape(1, width))


def per_device(
    D, M, tokens, attn_gain, w_query, key_w, value_w, w_out, final_gain, unembed,
    clean_ids, corrupt_ids,
):
    S = tokens.shape[0] // SEQUENCE_LENGTH
    vocab_rows, width = unembed.shape
    start = lax.axis_index("dp") * vocab_rows

    def picked(ids):
        at = ids - start
        ok = (at >= 0) & (at < vocab_rows)
        rows = jnp.take(unembed, jnp.clip(at, 0, vocab_rows - 1), axis=0)
        return jnp.where(ok[:, None], rows.astype(F32), 0.0)

    contrib = (picked(clean_ids) - picked(corrupt_ids)).reshape(D, S, width)
    qkv = project(D, M, tokens, attn_gain.reshape(1, -1), w_query, key_w, value_w)
    q_heads = w_query.shape[1] // HEAD_SIZE
    kv_heads = key_w.shape[1] // HEAD_SIZE
    head_out, stat = attend(qkv, q_heads, kv_heads)
    last_tokens = tokens.reshape(S, SEQUENCE_LENGTH, width)[:, SEQUENCE_LENGTH - 1, :]
    scores, metric = tail(
        D, M, stat, w_out, contrib, last_tokens, final_gain, tokens.shape[0] * D
    )
    return head_out, scores, metric.reshape(S)


def solution(mesh):
    in_specs = (
        P("dp", "mp"), P(), P("dp", "mp"), P("dp", "mp"), P("dp", "mp"),
        P("mp", "dp"), P("mp"), P("dp", "mp"), P(), P(),
    )
    out_specs = (P("dp", "mp"), P("dp", "mp"), P("dp"))
    return jax.shard_map(
        functools.partial(per_device, mesh.shape["dp"], mesh.shape["mp"]),
        mesh=mesh, in_specs=in_specs, out_specs=out_specs, check_vma=False,
    )
```

```python
import functools
import math

import jax
import jax.numpy as jnp
import numpy as np
from jax import lax
from jax.experimental import pallas as pl
from jax.experimental.pallas import tpu as pltpu
from jax.sharding import PartitionSpec as P

HEAD_SIZE = 128
SEQUENCE_LENGTH = 256
MESH = pl.DeviceIdType.MESH
F32 = jnp.float32
BF16 = jnp.bfloat16


def flip(index, mask):
    bit = 1
    out = index
    while bit <= mask:
        if mask & bit:
            out = out + bit - 2 * bit * ((index // bit) % 2)
        bit *= 2
    return out


def spread_plan(size):
    bits = []
    bit = 2
    while bit < size:
        bits.append(bit)
        bit *= 2
    parts = min(2, len(bits))
    plan = []
    for part in range(parts):
        order = bits[part:] + bits[:part]
        held = [0]
        arrivals = []
        for step, b in enumerate(order):
            fresh = [h ^ b for h in held]
            arrivals += [(f, step) for f in fresh]
            held = held + fresh
        plan.append((order, arrivals))
    return plan


def whole_kernel(
    D, M, chunks, xchunks, token_count,
    tok_ref, gain_ref, wq_ref, wk_ref, wv_ref, cos_hbm, sin_hbm, wout_hbm, contrib_ref, fgain_ref,
    head_ref, scores_ref, metric_ref,
    x_all, w_all, acc, cos_ref, sin_ref, wout_ref, tail_tok, q_s, k_s, v_s, tot_src,
    last_src, tot_all, last_all, rows_a, out_src, out_all, dir_all, sq_src, sq_all,
    g_src, g_all, hg_src, hg_all,
    loc_sem, one_sem, xs_sem, xr_sem, ps_sem, pr_sem, cs_sem, cr_sem,
    s1, r1, s2, r2, s3, r3, s4, r4, s5, r5, s6, r6, s7, r7,
):
    d = lax.axis_index("dp")
    m = lax.axis_index("mp")
    plan = spread_plan(D)
    parts = len(plan)
    depth = wq_ref.shape[0]
    rows, width = tok_ref.shape
    qw, kw, vw = wq_ref.shape[1], wk_ref.shape[1], wv_ref.shape[1]
    piece = depth // (parts * chunks)
    xpiece = rows // xchunks
    L = SEQUENCE_LENGTH
    S = rows // L
    heads, kv_heads = qw // HEAD_SIZE, kw // HEAD_SIZE
    G = heads // kv_heads
    cols = wout_ref.shape[1]
    R = D // M
    everyone = D * M
    me = d * M + m
    model_width = M * width

    def wrows(p, c):
        return pl.ds((p * chunks + c) * piece, piece)

    own = []
    for c in range(chunks):
        for p in range(parts):
            rr = wrows(p, c)
            trio = []
            for i, (src, lo, n) in enumerate(
                ((wq_ref, 0, qw), (wk_ref, qw, kw), (wv_ref, qw + kw, vw))
            ):
                cp = pltpu.make_async_copy(
                    src.at[rr, :], w_all.at[d, rr, pl.ds(lo, n)], loc_sem.at[p, c, i]
                )
                cp.start()
                trio.append(cp)
            own.append((p, c, trio))

    barrier = pltpu.get_barrier_semaphore()

    @pl.loop(1, everyone)
    def _(i):
        other = (me + i) % everyone
        pl.semaphore_signal(
            barrier, inc=1, device_id=(other // M, other % M), device_id_type=MESH
        )

    xown = pltpu.make_async_copy(tok_ref, x_all.at[m], one_sem.at[0])
    early = [
        pltpu.make_async_copy(cos_hbm, cos_ref, one_sem.at[1]),
        pltpu.make_async_copy(sin_hbm, sin_ref, one_sem.at[2]),
        pltpu.make_async_copy(wout_hbm, wout_ref, one_sem.at[3]),
    ]
    for b in range(S):
        early.append(pltpu.make_async_copy(
            tok_ref.at[pl.ds((b + 1) * L - 16, 16), :], tail_tok.at[b], one_sem.at[4 + b]
        ))
    pl.semaphore_wait(barrier, everyone - 1)

    pending = []

    def remote(src, dst, ss, rs, to, cond=None):
        cp = pltpu.make_async_remote_copy(
            src_ref=src, dst_ref=dst, send_sem=ss, recv_sem=rs, device_id=to, device_id_type=MESH
        )
        if cond is None:
            cp.start()
        else:
            pl.when(cond)(cp.start)
        pending.append((cp, cond))

    def local(src, dst, rs, cond=None):
        cp = pltpu.make_async_copy(src, dst, rs)
        if cond is None:
            cp.start()
        else:
            pl.when(cond)(cp.start)

    def arrive(buf, sem, n):
        for i in range(n):
            pltpu.make_async_copy(buf.at[i], buf.at[i], sem.at[i]).wait()

    def xsend(hop, c, side):
        rr = pl.ds(c * xpiece, xpiece)
        owner = m - hop if side == 0 else m + hop
        to = m + 1 if side == 0 else m - 1
        return pltpu.make_async_remote_copy(
            src_ref=(tok_ref.at[rr, :] if hop == 0 else x_all.at[owner, rr, :]),
            dst_ref=x_all.at[owner, rr, :],
            send_sem=xs_sem.at[hop, c, side],
            recv_sem=xr_sem.at[hop, c, side],
            device_id=(d, to),
            device_id_type=MESH,
        )

    def xpred(hop, side):
        if side == 0:
            return (m < M - 1) & (m - hop >= 0)
        return (m > 0) & (m + hop < M)

    def xstart(hop, c):
        for side in range(2):
            @pl.when(xpred(hop, side))
            def _(side=side):
                xsend(hop, c, side).start()

    def xwait(hop, c):
        rr = pl.ds(c * xpiece, xpiece)
        for side in range(2):
            owner = m - hop - 1 if side == 0 else m + hop + 1
            ok = (m - hop - 1 >= 0) if side == 0 else (m + hop + 1 < M)

            @pl.when(ok)
            def _(side=side, owner=owner):
                pltpu.make_async_copy(
                    x_all.at[owner, rr, :], x_all.at[owner, rr, :], xr_sem.at[hop, c, side]
                ).wait()

    def wcopy(mask, p, c, bit, send_sem, recv_sem):
        owner = flip(d, mask)
        rr = wrows(p, c)
        remote(w_all.at[owner, rr, :], w_all.at[owner, rr, :], send_sem, recv_sem,
               (flip(d, bit), m))

    def wsend(mask, p, c, step):
        bit = plan[p][0][step]
        wcopy(mask, p, c, bit, ps_sem.at[p, mask // 2, c, step],
              pr_sem.at[p, (mask ^ bit) // 2, c])

    def csend(mask, p, c):
        wcopy(mask, p, c, 1, cs_sem.at[p, mask // 2, c], cr_sem.at[p, mask // 2, c])

    def wwait(mask, p, c, sem):
        owner = flip(d, mask)
        rr = wrows(p, c)
        pltpu.make_async_copy(w_all.at[owner, rr, :], w_all.at[owner, rr, :], sem).wait()

    steps = len(plan[0][0])
    for i, (p, c, trio) in enumerate(own):
        for cp in trio:
            cp.wait()
        wsend(0, p, c, 0)
        if i == parts - 1:
            for cc in range(xchunks):
                xstart(0, cc)
    for step in range(1, steps):
        for c in range(chunks):
            for p in range(parts):
                wsend(0, p, c, step)
    for c in range(chunks):
        for p in range(parts):
            csend(0, p, c)
    xown.start()
    for cp in early:
        cp.start()
    for i in range(1, D):
        to = (d + i) % D
        remote(contrib_ref.at[to], dir_all.at[d], s2.at[i], r2.at[d], (to, m))
    local(contrib_ref.at[d], dir_all.at[d], r2.at[d])

    rounds = len(plan[0][1])
    wevents = [(r, c) for r in range(rounds) for c in range(chunks)]
    xevents = [(h, c) for h in range(M - 1) for c in range(xchunks)]
    merged = sorted(
        [((i + 1) / len(wevents), 1, e) for i, e in enumerate(wevents)]
        + [(0.8 * (i + 1) / len(xevents), 0, e) for i, e in enumerate(xevents)]
    )

    def use(owner, lo, n):
        base = owner * depth
        shard = base // width
        col = pl.multiple_of(base % width + lo, 128 if n % 128 == 0 else n)
        acc[...] += jnp.dot(
            x_all[shard, :, pl.ds(col, n)], w_all[owner, pl.ds(lo, n), :],
            preferred_element_type=F32,
        )

    every_piece = {(p, c) for p in range(parts) for c in range(chunks)}
    got = {0: set(every_piece)}
    used = set()
    late = []

    def sweep():
        whole = [k for k in got if got[k] == every_piece and not any((k, q) in used for q in every_piece)]
        for mask in whole:
            use(flip(d, mask), 0, depth)
        for mask in whole:
            for p, c in sorted(every_piece):
                wwait(mask + 1, p, c, cr_sem.at[p, mask // 2, c])
                used.add((mask, (p, c)))
            use(flip(d, mask + 1), 0, depth)
        fresh = sorted((k, q) for k in got for q in got[k] if (k, q) not in used)
        if piece % 128:
            fresh = []
        for mask, (p, c) in fresh:
            used.add((mask, (p, c)))
            use(flip(d, mask), (p * chunks + c) * piece, piece)
        finish()
        late.extend(fresh)

    def finish():
        for mask, (p, c) in late:
            wwait(mask + 1, p, c, cr_sem.at[p, mask // 2, c])
            use(flip(d, mask + 1), (p * chunks + c) * piece, piece)
        late.clear()

    x_left = len(xevents)
    for _, kind, (a, c) in merged:
        if kind == 0:
            xwait(a, c)
            if a + 1 < M - 1:
                xstart(a + 1, c)
            x_left -= 1
            if x_left == 0:
                xown.wait()
                total = jnp.zeros((rows, 1), F32)
                for k in range(M):
                    xv = x_all[k].astype(F32)
                    total = total + jnp.sum(xv * xv, axis=1, keepdims=True)
                inv = lax.rsqrt(total / model_width + 1e-05)
                for h in range(M - 1):
                    for cc in range(xchunks):
                        for side in range(2):
                            @pl.when(xpred(h, side))
                            def _(h=h, cc=cc, side=side):
                                xsend(h, cc, side).wait_send()
                for k in range(M):
                    g = gain_ref[:, k * width:(k + 1) * width].astype(F32)
                    x_all[k] = (x_all[k].astype(F32) * inv * g).astype(BF16)
                acc[...] = jnp.zeros_like(acc)
                sweep()
        else:
            for p in range(parts):
                mask, step = plan[p][1][a]
                wwait(mask, p, c, pr_sem.at[p, mask // 2, c])
                for later in range(step + 1, steps):
                    wsend(mask, p, c, later)
                csend(mask, p, c)
                got.setdefault(mask, set()).add((p, c))
            if x_left == 0:
                sweep()
    finish()

    for cp in early:
        cp.wait()
    half = HEAD_SIZE // 2

    def rope(x, cos, sin):
        turned = jnp.concatenate([x[:, half:], x[:, :half]], axis=1)
        return (x * cos + turned * sin).astype(BF16)

    def softmax(logits):
        e = jnp.exp(logits - jnp.max(logits, axis=1, keepdims=True))
        return (e / jnp.sum(e, axis=1, keepdims=True)).astype(BF16)

    def scaled(q, k):
        return lax.dot_general(
            q, k, (((1,), (1,)), ((), ())), preferred_element_type=F32
        ) / math.sqrt(HEAD_SIZE)

    for b in range(S):
        span_b = slice(b * L, (b + 1) * L)
        at_last = (b + 1) * L - 1
        for n in range(kv_heads):
            lo = qw + n * HEAD_SIZE
            k = rope(acc[span_b, lo:lo + HEAD_SIZE], cos_ref[...], sin_ref[...])
            v = acc[span_b, lo + kw:lo + kw + HEAD_SIZE].astype(BF16)
            k_s[b * kv_heads + n] = k
            v_s[b * kv_heads + n] = v
            for g in range(G):
                h = n * G + g
                q_s[g:g + 1, :] = acc[at_last:at_last + 1, h * HEAD_SIZE:(h + 1) * HEAD_SIZE]
            q = rope(q_s[...], cos_ref[L - 1:L, :], sin_ref[L - 1:L, :])
            mixed = jnp.dot(softmax(scaled(q, k)), v, preferred_element_type=F32)
            mixed = mixed.astype(BF16).astype(F32)
            for g in range(G):
                h = n * G + g
                last_src[b:b + 1, h * HEAD_SIZE:(h + 1) * HEAD_SIZE] = mixed[g:g + 1, :]
    for i in range(1, D):
        to = (d + i) % D
        remote(last_src, last_all.at[d], s1.at[i], r1.at[d], (to, m))
    local(last_src, last_all.at[d], r1.at[d])

    ahead = lax.broadcasted_iota(jnp.int32, (L, L), 0) >= lax.broadcasted_iota(jnp.int32, (L, L), 1)

    def attend(first, end):
        for b in range(S):
            @pl.loop(first, end)
            def _(h):
                at = pl.ds(pl.multiple_of(h * HEAD_SIZE, HEAD_SIZE), HEAD_SIZE)
                n = b * kv_heads + h // G
                q = rope(acc[pl.ds(b * L, L), at], cos_ref[...], sin_ref[...])
                logits = jnp.where(ahead, scaled(q, k_s[n]), -1e30)
                mixed = jnp.dot(softmax(logits), v_s[n], preferred_element_type=F32).astype(BF16)
                head_ref[pl.ds(b * L, L), at] = mixed
                column = jnp.sum(mixed.astype(F32), axis=0, keepdims=True)
                if b == 0:
                    tot_src[:, at] = column
                else:
                    tot_src[:, at] += column

    cut = heads * 3 // 8
    attend(0, cut)
    arrive(last_all, r1, D)
    for j in range(D):
        rows_a[j * S:(j + 1) * S, 0:qw] = last_all[j]
    w = wout_ref[...]
    partial = jnp.dot(rows_a[:, 0:qw].astype(BF16), w, preferred_element_type=F32)
    for j in range(D):
        out_src[j] = partial[j * S:(j + 1) * S, :]
    span = d // R
    slot = (d % R) * M + m
    for i in range(D):
        to = (d + i) % D
        if i == 0:
            remote(out_src.at[to], out_all.at[slot], s3.at[i], r3.at[slot], (to, span), m != span)
            local(out_src.at[to], out_all.at[slot], r3.at[slot], m == span)
        else:
            remote(out_src.at[to], out_all.at[slot], s3.at[i], r3.at[slot], (to, span))

    attend(cut, heads)
    for i in range(1, D):
        to = (d + i) % D
        remote(tot_src, tot_all.at[d], s4.at[i], r4.at[d], (to, m))
    local(tot_src, tot_all.at[d], r4.at[d])
    arrive(dir_all, r2, D)
    direction = dir_all[0]
    for j in range(1, D):
        direction = direction + dir_all[j]
    weighted = fgain_ref[...].astype(F32) * direction

    arrive(out_all, r3, D)
    pieces = []
    for jj in range(R):
        part_sum = out_all[jj * M]
        for k in range(1, M):
            part_sum = part_sum + out_all[jj * M + k]
        pieces.append(part_sum)
    attn_last = jnp.concatenate(pieces, axis=1).astype(BF16).astype(F32)
    toks = [tail_tok[b].astype(F32)[15:16, :] for b in range(S)]
    residual = (toks[0] if S == 1 else jnp.concatenate(toks, axis=0)) + attn_last
    sq_src[0] = jnp.broadcast_to(jnp.sum(residual * residual, axis=1, keepdims=True), (S, 128))
    sq_src[1] = jnp.broadcast_to(jnp.sum(residual * weighted, axis=1, keepdims=True), (S, 128))
    for i in range(1, M):
        to = (m + i) % M
        remote(sq_src, sq_all.at[m], s5.at[i], r5.at[m], (d, to))
    local(sq_src, sq_all.at[m], r5.at[m])
    arrive(sq_all, r5, M)
    square = sq_all[0, 0]
    product = sq_all[0, 1]
    for k in range(1, M):
        square = square + sq_all[k, 0]
        product = product + sq_all[k, 1]
    inverse = lax.rsqrt(square / model_width + 1e-05)
    metric = inverse * product
    metric_ref[...] = metric[:, 0:1]
    grad = weighted * inverse[:, 0:1] - residual * (
        metric * inverse * inverse / model_width
    )[:, 0:1]
    for jj in range(R):
        g_src[jj] = grad[:, jj * cols:(jj + 1) * cols].astype(BF16).astype(F32)
    for i in range(M - 1, -1, -1):
        k = (m + i) % M
        for jj in range(R):
            to = m * R + jj
            if i == 0:
                remote(g_src.at[jj], g_all.at[d], s6.at[jj, i], r6.at[d], (to, k), to != d)
                local(g_src.at[jj], g_all.at[d], r6.at[d], to == d)
            else:
                remote(g_src.at[jj], g_all.at[d], s6.at[jj, i], r6.at[d], (to, k))
    arrive(tot_all, r4, D)
    mean = tot_all[0]
    for j in range(1, D):
        mean = mean + tot_all[j]
    mean = mean / token_count
    arrive(g_all, r6, D)
    for j in range(D):
        rows_a[j * S:(j + 1) * S, 0:cols] = g_all[j]
    hg = lax.dot_general(
        rows_a[:, 0:cols].astype(BF16), w, (((1,), (1,)), ((), ())), preferred_element_type=F32
    )
    for j in range(D):
        hg_src[j] = hg[j * S:(j + 1) * S, :]
    for i in range(1, D):
        to = (d + i) % D
        remote(hg_src.at[to], hg_all.at[d], s7.at[i], r7.at[d], (to, m))
    local(hg_src.at[d], hg_all.at[d], r7.at[d])
    arrive(hg_all, r7, D)
    grads = hg_all[0]
    for j in range(1, D):
        grads = grads + hg_all[j]
    gap = (mean - last_src[...]) * grads
    lane = lax.broadcasted_iota(jnp.int32, (S, heads), 1)
    scores = jnp.zeros((S, heads), F32)
    for h in range(heads):
        part = jnp.sum(gap[:, h * HEAD_SIZE:(h + 1) * HEAD_SIZE], axis=1, keepdims=True)
        scores = jnp.where(lane == h, part, scores)
    scores_ref[...] = scores
    for cp, cond in pending:
        if cond is None:
            cp.wait_send()
        else:
            pl.when(cond)(cp.wait_send)


def tables():
    half = HEAD_SIZE // 2
    inv_freq = np.exp(np.arange(half) * (-2.0 * math.log(500000.0) / HEAD_SIZE))
    angles = np.arange(SEQUENCE_LENGTH)[:, None] * inv_freq[None, :]
    c, s = np.cos(angles), np.sin(angles)
    cos = np.concatenate([c, c], axis=1).astype(np.float32)
    return cos, np.concatenate([-s, s], axis=1).astype(np.float32)


def whole(D, M, tokens, gain, wq, wk, wv, w_out, contrib, final_gain):
    rows, width = tokens.shape
    S = rows // SEQUENCE_LENGTH
    depth = wq.shape[0]
    entries, cols = w_out.shape
    total = wq.shape[1] + wk.shape[1] + wv.shape[1]
    heads, kv_heads = wq.shape[1] // HEAD_SIZE, wk.shape[1] // HEAD_SIZE
    parts = len(spread_plan(D))
    steps = len(spread_plan(D)[0][0])
    chunks = max(1, min(4, depth // (128 * parts)))
    xchunks = 2
    half = D // 2
    R = D // M
    cos, sin = tables()
    DMA = pltpu.SemaphoreType.DMA
    ANY = pl.BlockSpec(memory_space=pl.ANY)
    V = pl.BlockSpec(memory_space=pltpu.VMEM)

    def f(*shape):
        return pltpu.VMEM(shape, F32)

    def h(*shape):
        return pltpu.VMEM(shape, BF16)

    return pl.pallas_call(
        functools.partial(whole_kernel, D, M, chunks, xchunks, rows * D),
        name="whole",
        out_shape=[
            jax.ShapeDtypeStruct((rows, entries), BF16),
            jax.ShapeDtypeStruct((S, heads), F32),
            jax.ShapeDtypeStruct((S, 1), F32),
        ],
        in_specs=[ANY, V, ANY, ANY, ANY, ANY, ANY, ANY, ANY, V],
        out_specs=[V, V, V],
        scratch_shapes=[
            h(M, rows, width), h(D, depth, total), f(rows, total),
            f(SEQUENCE_LENGTH, HEAD_SIZE), f(SEQUENCE_LENGTH, HEAD_SIZE),
            h(entries, cols), h(S, 16, width), f(heads // kv_heads, HEAD_SIZE),
            h(S * kv_heads, SEQUENCE_LENGTH, HEAD_SIZE), h(S * kv_heads, SEQUENCE_LENGTH, HEAD_SIZE),
            f(1, entries), f(S, entries), f(D, 1, entries), f(D, S, entries),
            f(D * S, max(entries, cols)), f(D, S, cols), f(D, S, cols), f(D, S, width),
            f(2, S, 128), f(M, 2, S, 128), f(R, S, cols), f(D, S, cols),
            f(D, S, entries), f(D, S, entries),
            DMA((parts, chunks, 3)), DMA((4 + S,)),
            DMA((M - 1, xchunks, 2)), DMA((M - 1, xchunks, 2)),
            DMA((parts, half, chunks, steps)), DMA((parts, half, chunks)),
            DMA((parts, half, chunks)), DMA((parts, half, chunks)),
            DMA((D,)), DMA((D,)), DMA((D,)), DMA((D,)), DMA((D,)), DMA((D,)), DMA((D,)), DMA((D,)),
            DMA((M,)), DMA((M,)), DMA((R, M)), DMA((D,)), DMA((D,)), DMA((D,)),
        ],
        compiler_params=pltpu.CompilerParams(
            collective_id=0, has_side_effects=True, vmem_limit_bytes=56 * 1024 * 1024
        ),
    )(tokens, gain, wq, wk, wv, jnp.asarray(cos), jnp.asarray(sin), w_out, contrib,
      final_gain.reshape(1, width))


GROUP = 16


def pick_kernel(per, at_ref, *refs):
    blocks, out_ref = refs[:-1], refs[-1]
    step = pl.program_id(0)
    total = pl.num_programs(0) * per
    where = lax.broadcasted_iota(jnp.int32, (GROUP, 1), 0)
    for i in range(per):
        rows = []
        for side in range(2):
            at = at_ref[side * total + step * per + i]
            block = blocks[side * per + i][...].astype(F32)
            hit = (where == at % GROUP) & (at >= 0)
            rows.append(jnp.sum(jnp.where(hit, block, 0.0), axis=0, keepdims=True))
        out_ref[i] = rows[0] - rows[1]


def pick(unembed, at):
    width = unembed.shape[1]
    n = at.shape[0] // 2
    per = min(8, n)

    def spec(side, i):
        def index(step, at_ref):
            return jnp.maximum(at_ref[side * n + step * per + i], 0) // GROUP, 0
        return pl.BlockSpec((GROUP, width), index)

    return pl.pallas_call(
        functools.partial(pick_kernel, per),
        name="pick",
        grid_spec=pltpu.PrefetchScalarGridSpec(
            num_scalar_prefetch=1,
            grid=(n // per,),
            in_specs=[spec(side, i) for side in range(2) for i in range(per)],
            out_specs=pl.BlockSpec((per, 1, width), lambda step, at_ref: (step, 0, 0)),
        ),
        out_shape=jax.ShapeDtypeStruct((n, 1, width), F32),
    )(at, *([unembed] * (2 * per)))


def per_device(
    D, M, tokens, attn_gain, w_query, key_w, value_w, w_out, final_gain, unembed,
    clean_ids, corrupt_ids,
):
    S = tokens.shape[0] // SEQUENCE_LENGTH
    vocab_rows, width = unembed.shape
    at = jnp.concatenate([clean_ids, corrupt_ids]) - lax.axis_index("dp") * vocab_rows
    at = jnp.where(at < vocab_rows, jnp.maximum(at, -1), -1)
    contrib = pick(unembed, at).reshape(D, S, width)
    head_out, scores, metric = whole(
        D, M, tokens, attn_gain.reshape(1, -1), w_query, key_w, value_w, w_out, contrib, final_gain
    )
    return head_out, scores, metric.reshape(S)


def solution(mesh):
    in_specs = (
        P("dp", "mp"), P(), P("dp", "mp"), P("dp", "mp"), P("dp", "mp"),
        P("mp", "dp"), P("mp"), P("dp", "mp"), P(), P(),
    )
    out_specs = (P("dp", "mp"), P("dp", "mp"), P("dp"))
    return jax.shard_map(
        functools.partial(per_device, mesh.shape["dp"], mesh.shape["mp"]),
        mesh=mesh, in_specs=in_specs, out_specs=out_specs, check_vma=False,
    )
```

```python
import functools
import math

import jax
import jax.numpy as jnp
import numpy as np
from jax import lax
from jax.experimental import pallas as pl
from jax.experimental.pallas import tpu as pltpu
from jax.sharding import PartitionSpec as P

HEAD_SIZE = 128
SEQUENCE_LENGTH = 256
MESH = pl.DeviceIdType.MESH
F32 = jnp.float32
BF16 = jnp.bfloat16


def flip(index, mask):
    bit = 1
    out = index
    while bit <= mask:
        if mask & bit:
            out = out + bit - 2 * bit * ((index // bit) % 2)
        bit *= 2
    return out


def spread_plan(size):
    bits = []
    bit = 2
    while bit < size:
        bits.append(bit)
        bit *= 2
    parts = min(2, len(bits))
    plan = []
    for part in range(parts):
        order = bits[part:] + bits[:part]
        held = [0]
        arrivals = []
        for step, b in enumerate(order):
            fresh = [h ^ b for h in held]
            arrivals += [(f, step) for f in fresh]
            held = held + fresh
        plan.append((order, arrivals))
    return plan


def whole_kernel(
    D, M, chunks, xchunks, token_count,
    tok_ref, gain_ref, wq_ref, wk_ref, wv_ref, cos_hbm, sin_hbm, wout_hbm, contrib_ref, fgain_ref,
    head_ref, scores_ref, metric_ref,
    x_all, w_all, acc, cos_ref, sin_ref, wout_ref, tail_tok, q_s, k_s, v_s, tot_src,
    last_src, tot_all, last_all, rows_a, out_src, out_all, dir_all, sq_src, sq_all,
    g_src, g_all, hg_src, hg_all, rows_g,
    loc_sem, one_sem, xs_sem, xr_sem, ps_sem, pr_sem, cs_sem, cr_sem,
    s1, r1, s2, r2, s3, r3, s4, r4, s5, r5, s6, r6, s7, r7,
):
    d = lax.axis_index("dp")
    m = lax.axis_index("mp")
    plan = spread_plan(D)
    parts = len(plan)
    depth = wq_ref.shape[0]
    rows, width = tok_ref.shape
    qw, kw, vw = wq_ref.shape[1], wk_ref.shape[1], wv_ref.shape[1]
    piece = depth // (parts * chunks)
    xpiece = rows // xchunks
    L = SEQUENCE_LENGTH
    S = rows // L
    heads, kv_heads = qw // HEAD_SIZE, kw // HEAD_SIZE
    G = heads // kv_heads
    cols = wout_ref.shape[1]
    R = D // M
    everyone = D * M
    me = d * M + m
    model_width = M * width

    def wrows(p, c):
        return pl.ds((p * chunks + c) * piece, piece)

    own = []
    for c in range(chunks):
        for p in range(parts):
            rr = wrows(p, c)
            trio = []
            for i, (src, lo, n) in enumerate(
                ((wq_ref, 0, qw), (wk_ref, qw, kw), (wv_ref, qw + kw, vw))
            ):
                cp = pltpu.make_async_copy(
                    src.at[rr, :], w_all.at[d, rr, pl.ds(lo, n)], loc_sem.at[p, c, i]
                )
                cp.start()
                trio.append(cp)
            own.append((p, c, trio))

    barrier = pltpu.get_barrier_semaphore()

    @pl.loop(1, everyone)
    def _(i):
        other = (me + i) % everyone
        pl.semaphore_signal(
            barrier, inc=1, device_id=(other // M, other % M), device_id_type=MESH
        )

    xown = pltpu.make_async_copy(tok_ref, x_all.at[m], one_sem.at[0])
    early = [
        pltpu.make_async_copy(cos_hbm, cos_ref, one_sem.at[1]),
        pltpu.make_async_copy(sin_hbm, sin_ref, one_sem.at[2]),
        pltpu.make_async_copy(wout_hbm, wout_ref, one_sem.at[3]),
    ]
    for b in range(S):
        early.append(pltpu.make_async_copy(
            tok_ref.at[pl.ds((b + 1) * L - 16, 16), :], tail_tok.at[b], one_sem.at[4 + b]
        ))
    pl.semaphore_wait(barrier, everyone - 1)

    pending = []

    def remote(src, dst, ss, rs, to, cond=None):
        cp = pltpu.make_async_remote_copy(
            src_ref=src, dst_ref=dst, send_sem=ss, recv_sem=rs, device_id=to, device_id_type=MESH
        )
        if cond is None:
            cp.start()
        else:
            pl.when(cond)(cp.start)
        pending.append((cp, cond))

    def local(src, dst, rs, cond=None):
        cp = pltpu.make_async_copy(src, dst, rs)
        if cond is None:
            cp.start()
        else:
            pl.when(cond)(cp.start)

    def arrive(buf, sem, n):
        for i in range(n):
            pltpu.make_async_copy(buf.at[i], buf.at[i], sem.at[i]).wait()

    def xsend(hop, c, side):
        rr = pl.ds(c * xpiece, xpiece)
        owner = m - hop if side == 0 else m + hop
        to = m + 1 if side == 0 else m - 1
        return pltpu.make_async_remote_copy(
            src_ref=(tok_ref.at[rr, :] if hop == 0 else x_all.at[owner, rr, :]),
            dst_ref=x_all.at[owner, rr, :],
            send_sem=xs_sem.at[hop, c, side],
            recv_sem=xr_sem.at[hop, c, side],
            device_id=(d, to),
            device_id_type=MESH,
        )

    def xpred(hop, side):
        if side == 0:
            return (m < M - 1) & (m - hop >= 0)
        return (m > 0) & (m + hop < M)

    def xstart(hop, c):
        for side in range(2):
            @pl.when(xpred(hop, side))
            def _(side=side):
                xsend(hop, c, side).start()

    def xwait(hop, c):
        rr = pl.ds(c * xpiece, xpiece)
        for side in range(2):
            owner = m - hop - 1 if side == 0 else m + hop + 1
            ok = (m - hop - 1 >= 0) if side == 0 else (m + hop + 1 < M)

            @pl.when(ok)
            def _(side=side, owner=owner):
                pltpu.make_async_copy(
                    x_all.at[owner, rr, :], x_all.at[owner, rr, :], xr_sem.at[hop, c, side]
                ).wait()

    def wcopy(mask, p, c, bit, send_sem, recv_sem):
        owner = flip(d, mask)
        rr = wrows(p, c)
        remote(w_all.at[owner, rr, :], w_all.at[owner, rr, :], send_sem, recv_sem,
               (flip(d, bit), m))

    def wsend(mask, p, c, step):
        bit = plan[p][0][step]
        wcopy(mask, p, c, bit, ps_sem.at[p, mask // 2, c, step],
              pr_sem.at[p, (mask ^ bit) // 2, c])

    def csend(mask, p, c):
        wcopy(mask, p, c, 1, cs_sem.at[p, mask // 2, c], cr_sem.at[p, mask // 2, c])

    def wwait(mask, p, c, sem):
        owner = flip(d, mask)
        rr = wrows(p, c)
        pltpu.make_async_copy(w_all.at[owner, rr, :], w_all.at[owner, rr, :], sem).wait()

    steps = len(plan[0][0])
    for i, (p, c, trio) in enumerate(own):
        for cp in trio:
            cp.wait()
        wsend(0, p, c, 0)
        if i == parts - 1:
            for cc in range(xchunks):
                xstart(0, cc)
    for step in range(1, steps):
        for c in range(chunks):
            for p in range(parts):
                wsend(0, p, c, step)
    for c in range(chunks):
        for p in range(parts):
            csend(0, p, c)
    xown.start()
    for cp in early:
        cp.start()
    for i in range(1, D):
        to = (d + i) % D
        remote(contrib_ref.at[to], dir_all.at[d], s2.at[i], r2.at[d], (to, m))
    local(contrib_ref.at[d], dir_all.at[d], r2.at[d])

    rounds = len(plan[0][1])
    wevents = [(r, c) for r in range(rounds) for c in range(chunks)]
    xevents = [(h, c) for h in range(M - 1) for c in range(xchunks)]
    merged = sorted(
        [((i + 1) / len(wevents), 1, e) for i, e in enumerate(wevents)]
        + [(0.8 * (i + 1) / len(xevents), 0, e) for i, e in enumerate(xevents)]
    )

    def use(owner, lo, n):
        base = owner * depth
        shard = base // width
        col = pl.multiple_of(base % width + lo, 128 if n % 128 == 0 else n)
        acc[...] += jnp.dot(
            x_all[shard, :, pl.ds(col, n)], w_all[owner, pl.ds(lo, n), :],
            preferred_element_type=F32,
        )

    every_piece = {(p, c) for p in range(parts) for c in range(chunks)}
    got = {0: set(every_piece)}
    used = set()
    late = []
    todo = []

    def sweep(left):
        whole = [k for k in got if got[k] == every_piece and not any((k, q) in used for q in every_piece)]
        for mask in whole:
            todo.append((mask, False))
            used.update((mask, q) for q in every_piece)
        todo.extend((mask, True) for mask in whole)
        fresh = sorted((k, q) for k in got for q in got[k] if (k, q) not in used)
        if piece % 128:
            fresh = []
        for mask, (p, c) in fresh:
            used.add((mask, (p, c)))
            use(flip(d, mask), (p * chunks + c) * piece, piece)
        finish()
        late.extend(fresh)
        drain(-(-len(todo) // max(1, left - 1)))

    def drain(n):
        for mask, paired in todo[:n]:
            if paired:
                for p, c in sorted(every_piece):
                    wwait(mask + 1, p, c, cr_sem.at[p, mask // 2, c])
            use(flip(d, mask + int(paired)), 0, depth)
        del todo[:n]

    def finish():
        for mask, (p, c) in late:
            wwait(mask + 1, p, c, cr_sem.at[p, mask // 2, c])
            use(flip(d, mask + 1), (p * chunks + c) * piece, piece)
        late.clear()

    x_left = len(xevents)
    for _, kind, (a, c) in merged:
        if kind == 0:
            xwait(a, c)
            if a + 1 < M - 1:
                xstart(a + 1, c)
            x_left -= 1
            if x_left == 0:
                xown.wait()
                total = jnp.zeros((rows, 1), F32)
                for k in range(M):
                    xv = x_all[k].astype(F32)
                    total = total + jnp.sum(xv * xv, axis=1, keepdims=True)
                inv = lax.rsqrt(total / model_width + 1e-05)
                for h in range(M - 1):
                    for cc in range(xchunks):
                        for side in range(2):
                            @pl.when(xpred(h, side))
                            def _(h=h, cc=cc, side=side):
                                xsend(h, cc, side).wait_send()
                for k in range(M):
                    g = gain_ref[k * width:(k + 1) * width].astype(F32).reshape(1, width)
                    x_all[k] = (x_all[k].astype(F32) * inv * g).astype(BF16)
                acc[...] = jnp.zeros_like(acc)
        else:
            for p in range(parts):
                mask, step = plan[p][1][a]
                wwait(mask, p, c, pr_sem.at[p, mask // 2, c])
                for later in range(step + 1, steps):
                    wsend(mask, p, c, later)
                csend(mask, p, c)
                got.setdefault(mask, set()).add((p, c))
            if x_left == 0:
                sweep(len(wevents) - wevents.index((a, c)))
    drain(len(todo))
    finish()

    for cp in early:
        cp.wait()
    half = HEAD_SIZE // 2

    def rope(x, cos, sin):
        turned = jnp.concatenate([x[:, half:], x[:, :half]], axis=1)
        return (x * cos + turned * sin).astype(BF16)

    def softmax(logits):
        e = jnp.exp(logits - jnp.max(logits, axis=1, keepdims=True))
        return (e / jnp.sum(e, axis=1, keepdims=True)).astype(BF16)

    def scaled(q, k):
        return lax.dot_general(
            q, k, (((1,), (1,)), ((), ())), preferred_element_type=F32
        ) / math.sqrt(HEAD_SIZE)

    for b in range(S):
        span_b = slice(b * L, (b + 1) * L)
        at_last = (b + 1) * L - 1
        for n in range(kv_heads):
            lo = qw + n * HEAD_SIZE
            k = rope(acc[span_b, lo:lo + HEAD_SIZE], cos_ref[...], sin_ref[...])
            v = acc[span_b, lo + kw:lo + kw + HEAD_SIZE].astype(BF16)
            k_s[b * kv_heads + n] = k
            v_s[b * kv_heads + n] = v
            for g in range(G):
                h = n * G + g
                q_s[g:g + 1, :] = acc[at_last:at_last + 1, h * HEAD_SIZE:(h + 1) * HEAD_SIZE]
            q = rope(q_s[...], cos_ref[L - 1:L, :], sin_ref[L - 1:L, :])
            mixed = jnp.dot(softmax(scaled(q, k)), v, preferred_element_type=F32)
            mixed = mixed.astype(BF16).astype(F32)
            for g in range(G):
                h = n * G + g
                last_src[b:b + 1, h * HEAD_SIZE:(h + 1) * HEAD_SIZE] = mixed[g:g + 1, :]
    for i in range(1, D):
        to = (d + i) % D
        remote(last_src, last_all.at[d], s1.at[i], r1.at[d], (to, m))
    local(last_src, last_all.at[d], r1.at[d])

    ahead = lax.broadcasted_iota(jnp.int32, (L, L), 0) >= lax.broadcasted_iota(jnp.int32, (L, L), 1)

    def attend(first, end):
        for b in range(S):
            @pl.loop(first, end)
            def _(h):
                at = pl.ds(pl.multiple_of(h * HEAD_SIZE, HEAD_SIZE), HEAD_SIZE)
                n = b * kv_heads + h // G
                q = rope(acc[pl.ds(b * L, L), at], cos_ref[...], sin_ref[...])
                logits = jnp.where(ahead, scaled(q, k_s[n]), -1e30)
                mixed = jnp.dot(softmax(logits), v_s[n], preferred_element_type=F32).astype(BF16)
                head_ref[pl.ds(b * L, L), at] = mixed
                column = jnp.sum(mixed.astype(F32), axis=0, keepdims=True)
                if b == 0:
                    tot_src[:, at] = column
                else:
                    tot_src[:, at] += column

    cut = heads * 3 // 8
    attend(0, cut)
    arrive(last_all, r1, D)
    for j in range(D):
        rows_a[j * S:(j + 1) * S, 0:qw] = last_all[j]
    w = wout_ref[...]
    partial = jnp.dot(rows_a[:, 0:qw].astype(BF16), w, preferred_element_type=F32)
    for j in range(D):
        out_src[j] = partial[j * S:(j + 1) * S, :]
    span = d // R
    slot = (d % R) * M + m
    for i in range(D):
        to = (d + i) % D
        if i == 0:
            remote(out_src.at[to], out_all.at[slot], s3.at[i], r3.at[slot], (to, span), m != span)
            local(out_src.at[to], out_all.at[slot], r3.at[slot], m == span)
        else:
            remote(out_src.at[to], out_all.at[slot], s3.at[i], r3.at[slot], (to, span))

    attend(cut, heads)
    for i in range(1, D):
        to = (d + i) % D
        remote(tot_src, tot_all.at[d], s4.at[i], r4.at[d], (to, m))
    local(tot_src, tot_all.at[d], r4.at[d])
    arrive(dir_all, r2, D)
    direction = dir_all[0]
    for j in range(1, D):
        direction = direction + dir_all[j]
    weighted = fgain_ref[...].astype(F32).reshape(1, width) * direction

    arrive(out_all, r3, D)
    pieces = []
    for jj in range(R):
        part_sum = out_all[jj * M]
        for k in range(1, M):
            part_sum = part_sum + out_all[jj * M + k]
        pieces.append(part_sum)
    attn_last = jnp.concatenate(pieces, axis=1).astype(BF16).astype(F32)
    toks = [tail_tok[b].astype(F32)[15:16, :] for b in range(S)]
    residual = (toks[0] if S == 1 else jnp.concatenate(toks, axis=0)) + attn_last
    sq_src[0] = jnp.broadcast_to(jnp.sum(residual * residual, axis=1, keepdims=True), (S, 128))
    sq_src[1] = jnp.broadcast_to(jnp.sum(residual * weighted, axis=1, keepdims=True), (S, 128))
    for i in range(1, M):
        to = (m + i) % M
        remote(sq_src, sq_all.at[m], s5.at[i], r5.at[m], (d, to))
    local(sq_src, sq_all.at[m], r5.at[m])
    for jj in range(R):
        g_src[jj, 0:S, :] = weighted[:, jj * cols:(jj + 1) * cols]
        g_src[jj, S:2 * S, :] = residual[:, jj * cols:(jj + 1) * cols]
    for i in range(M - 1, -1, -1):
        k = (m + i) % M
        for jj in range(R):
            to = m * R + jj
            if i == 0:
                remote(g_src.at[jj], g_all.at[d], s6.at[jj, i], r6.at[d], (to, k), to != d)
                local(g_src.at[jj], g_all.at[d], r6.at[d], to == d)
            else:
                remote(g_src.at[jj], g_all.at[d], s6.at[jj, i], r6.at[d], (to, k))
    arrive(sq_all, r5, M)
    square = sq_all[0, 0]
    product = sq_all[0, 1]
    for k in range(1, M):
        square = square + sq_all[k, 0]
        product = product + sq_all[k, 1]
    inverse = lax.rsqrt(square / model_width + 1e-05)
    metric = inverse * product
    metric_ref[...] = metric[:, 0:1]
    fall = (metric * inverse * inverse / model_width)[:, 0:1]
    arrive(tot_all, r4, D)
    mean = tot_all[0]
    for j in range(1, D):
        mean = mean + tot_all[j]
    mean = mean / token_count
    arrive(g_all, r6, D)
    for j in range(D):
        rows_g[2 * j * S:2 * (j + 1) * S, :] = g_all[j]
    exact = rows_g[...]
    coarse = exact.astype(BF16)
    fine = (exact - coarse.astype(F32)).astype(BF16)
    both = lax.dot_general(
        jnp.concatenate([coarse, fine], axis=0), w, (((1,), (1,)), ((), ())),
        preferred_element_type=F32,
    )
    hg = both[:2 * D * S] + both[2 * D * S:]
    for j in range(D):
        hg_src[j] = hg[2 * j * S:2 * (j + 1) * S, :]
    for i in range(1, D):
        to = (d + i) % D
        remote(hg_src.at[to], hg_all.at[d], s7.at[i], r7.at[d], (to, m))
    local(hg_src.at[d], hg_all.at[d], r7.at[d])
    arrive(hg_all, r7, D)
    joint = hg_all[0]
    for j in range(1, D):
        joint = joint + hg_all[j]
    grads = joint[0:S] * inverse[:, 0:1] - joint[S:2 * S] * fall
    gap = (mean - last_src[...]) * grads
    lane = lax.broadcasted_iota(jnp.int32, (S, heads), 1)
    scores = jnp.zeros((S, heads), F32)
    for h in range(heads):
        part = jnp.sum(gap[:, h * HEAD_SIZE:(h + 1) * HEAD_SIZE], axis=1, keepdims=True)
        scores = jnp.where(lane == h, part, scores)
    scores_ref[...] = scores
    for cp, cond in pending:
        if cond is None:
            cp.wait_send()
        else:
            pl.when(cond)(cp.wait_send)


def tables():
    half = HEAD_SIZE // 2
    inv_freq = np.exp(np.arange(half) * (-2.0 * math.log(500000.0) / HEAD_SIZE))
    angles = np.arange(SEQUENCE_LENGTH)[:, None] * inv_freq[None, :]
    c, s = np.cos(angles), np.sin(angles)
    cos = np.concatenate([c, c], axis=1).astype(np.float32)
    return cos, np.concatenate([-s, s], axis=1).astype(np.float32)


def whole(D, M, tokens, gain, wq, wk, wv, w_out, contrib, final_gain):
    rows, width = tokens.shape
    S = rows // SEQUENCE_LENGTH
    depth = wq.shape[0]
    entries, cols = w_out.shape
    total = wq.shape[1] + wk.shape[1] + wv.shape[1]
    heads, kv_heads = wq.shape[1] // HEAD_SIZE, wk.shape[1] // HEAD_SIZE
    parts = len(spread_plan(D))
    steps = len(spread_plan(D)[0][0])
    chunks = max(1, min(4, depth // (128 * parts)))
    xchunks = 2
    half = D // 2
    R = D // M
    cos, sin = tables()
    DMA = pltpu.SemaphoreType.DMA
    ANY = pl.BlockSpec(memory_space=pl.ANY)
    V = pl.BlockSpec(memory_space=pltpu.VMEM)

    def f(*shape):
        return pltpu.VMEM(shape, F32)

    def h(*shape):
        return pltpu.VMEM(shape, BF16)

    return pl.pallas_call(
        functools.partial(whole_kernel, D, M, chunks, xchunks, rows * D),
        name="whole",
        out_shape=[
            jax.ShapeDtypeStruct((rows, entries), BF16),
            jax.ShapeDtypeStruct((S, heads), F32),
            jax.ShapeDtypeStruct((S, 1), F32),
        ],
        in_specs=[ANY, V, ANY, ANY, ANY, ANY, ANY, ANY, ANY, V],
        out_specs=[V, V, V],
        scratch_shapes=[
            h(M, rows, width), h(D, depth, total), f(rows, total),
            f(SEQUENCE_LENGTH, HEAD_SIZE), f(SEQUENCE_LENGTH, HEAD_SIZE),
            h(entries, cols), h(S, 16, width), f(heads // kv_heads, HEAD_SIZE),
            h(S * kv_heads, SEQUENCE_LENGTH, HEAD_SIZE), h(S * kv_heads, SEQUENCE_LENGTH, HEAD_SIZE),
            f(1, entries), f(S, entries), f(D, 1, entries), f(D, S, entries),
            f(D * S, max(entries, cols)), f(D, S, cols), f(D, S, cols), f(D, S, width),
            f(2, S, 128), f(M, 2, S, 128), f(R, 2 * S, cols), f(D, 2 * S, cols),
            f(D, 2 * S, entries), f(D, 2 * S, entries), f(2 * D * S, cols),
            DMA((parts, chunks, 3)), DMA((4 + S,)),
            DMA((M - 1, xchunks, 2)), DMA((M - 1, xchunks, 2)),
            DMA((parts, half, chunks, steps)), DMA((parts, half, chunks)),
            DMA((parts, half, chunks)), DMA((parts, half, chunks)),
            DMA((D,)), DMA((D,)), DMA((D,)), DMA((D,)), DMA((D,)), DMA((D,)), DMA((D,)), DMA((D,)),
            DMA((M,)), DMA((M,)), DMA((R, M)), DMA((D,)), DMA((D,)), DMA((D,)),
        ],
        compiler_params=pltpu.CompilerParams(
            collective_id=0, has_side_effects=True, vmem_limit_bytes=56 * 1024 * 1024
        ),
    )(tokens, gain, wq, wk, wv, jnp.asarray(cos), jnp.asarray(sin), w_out, contrib,
      final_gain)


GROUP = 16


def pick_kernel(per, vocab_rows, clean_ref, corrupt_ref, *refs):
    blocks, out_ref = refs[:-1], refs[-1]
    step = pl.program_id(0)
    start = lax.axis_index("dp") * vocab_rows
    where = lax.broadcasted_iota(jnp.int32, (GROUP, 1), 0)
    for i in range(per):
        rows = []
        for side in range(2):
            at = (clean_ref, corrupt_ref)[side][step * per + i] - start
            block = blocks[side * per + i][...].astype(F32)
            hit = (where == at % GROUP) & (at >= 0) & (at < vocab_rows)
            rows.append(jnp.sum(jnp.where(hit, block, 0.0), axis=0, keepdims=True))
        out_ref[i] = rows[0] - rows[1]


def pick(unembed, clean_ids, corrupt_ids):
    vocab_rows, width = unembed.shape
    n = clean_ids.shape[0]
    per = min(8, n)

    def spec(side, i):
        def index(step, *ids):
            at = ids[side][step * per + i] - lax.axis_index("dp") * vocab_rows
            return jnp.clip(at, 0, vocab_rows - 1) // GROUP, 0
        return pl.BlockSpec((GROUP, width), index)

    return pl.pallas_call(
        functools.partial(pick_kernel, per, vocab_rows),
        name="pick",
        grid_spec=pltpu.PrefetchScalarGridSpec(
            num_scalar_prefetch=2,
            grid=(n // per,),
            in_specs=[spec(side, i) for side in range(2) for i in range(per)],
            out_specs=pl.BlockSpec((per, 1, width), lambda step, *ids: (step, 0, 0)),
        ),
        out_shape=jax.ShapeDtypeStruct((n, 1, width), F32),
    )(clean_ids, corrupt_ids, *([unembed] * (2 * per)))


def per_device(
    D, M, tokens, attn_gain, w_query, key_w, value_w, w_out, final_gain, unembed,
    clean_ids, corrupt_ids,
):
    S = tokens.shape[0] // SEQUENCE_LENGTH
    width = unembed.shape[1]
    contrib = pick(unembed, clean_ids, corrupt_ids).reshape(D, S, width)
    head_out, scores, metric = whole(
        D, M, tokens, attn_gain, w_query, key_w, value_w, w_out, contrib, final_gain
    )
    return head_out, scores, metric.reshape(S)


def solution(mesh):
    in_specs = (
        P("dp", "mp"), P(), P("dp", "mp"), P("dp", "mp"), P("dp", "mp"),
        P("mp", "dp"), P("mp"), P("dp", "mp"), P(), P(),
    )
    out_specs = (P("dp", "mp"), P("dp", "mp"), P("dp"))
    return jax.shard_map(
        functools.partial(per_device, mesh.shape["dp"], mesh.shape["mp"]),
        mesh=mesh, in_specs=in_specs, out_specs=out_specs, check_vma=False,
    )
```

```python
import functools
import math

import jax
import jax.numpy as jnp
import numpy as np
from jax import lax
from jax.experimental import pallas as pl
from jax.experimental.pallas import tpu as pltpu
from jax.sharding import PartitionSpec as P

HEAD_SIZE = 128
SEQUENCE_LENGTH = 256
MESH = pl.DeviceIdType.MESH
F32 = jnp.float32
BF16 = jnp.bfloat16


def flip(index, mask):
    bit = 1
    out = index
    while bit <= mask:
        if mask & bit:
            out = out + bit - 2 * bit * ((index // bit) % 2)
        bit *= 2
    return out


def spread_plan(size):
    bits = []
    bit = 2
    while bit < size:
        bits.append(bit)
        bit *= 2
    parts = min(2, len(bits))
    plan = []
    for part in range(parts):
        order = bits[part:] + bits[:part]
        held = [0]
        arrivals = []
        for step, b in enumerate(order):
            fresh = [h ^ b for h in held]
            arrivals += [(f, step) for f in fresh]
            held = held + fresh
        plan.append((order, arrivals))
    return plan


def whole_kernel(
    D, M, chunks, xchunks, token_count,
    tok_ref, gain_ref, wq_ref, wk_ref, wv_ref, cos_hbm, sin_hbm, wout_hbm, contrib_ref, fgain_ref,
    head_ref, scores_ref, metric_ref,
    x_all, w_all, acc, cos_ref, sin_ref, wout_ref, tail_tok, q_s, k_s, v_s, tot_src,
    last_src, tot_all, last_all, rows_a, out_src, out_all, dir_all, sq_src, sq_all,
    g_src, g_all, hg_src, hg_all, rows_g,
    loc_sem, one_sem, xs_sem, xr_sem, ps_sem, pr_sem, cs_sem, cr_sem,
    s1, r1, s2, r2, s3, r3, s4, r4, s5, r5, s6, r6, s7, r7,
):
    d = lax.axis_index("dp")
    m = lax.axis_index("mp")
    plan = spread_plan(D)
    parts = len(plan)
    depth = wq_ref.shape[0]
    rows, width = tok_ref.shape
    qw, kw, vw = wq_ref.shape[1], wk_ref.shape[1], wv_ref.shape[1]
    piece = depth // (parts * chunks)
    xpiece = rows // xchunks
    L = SEQUENCE_LENGTH
    S = rows // L
    heads, kv_heads = qw // HEAD_SIZE, kw // HEAD_SIZE
    G = heads // kv_heads
    cols = wout_ref.shape[1]
    R = D // M
    everyone = D * M
    me = d * M + m
    model_width = M * width

    def wrows(p, c):
        return pl.ds((p * chunks + c) * piece, piece)

    own = []
    for c in range(chunks):
        for p in range(parts):
            rr = wrows(p, c)
            trio = []
            for i, (src, lo, n) in enumerate(
                ((wq_ref, 0, qw), (wk_ref, qw, kw), (wv_ref, qw + kw, vw))
            ):
                cp = pltpu.make_async_copy(
                    src.at[rr, :], w_all.at[d, rr, pl.ds(lo, n)], loc_sem.at[p, c, i]
                )
                cp.start()
                trio.append(cp)
            own.append((p, c, trio))

    barrier = pltpu.get_barrier_semaphore()

    @pl.loop(1, everyone)
    def _(i):
        other = (me + i) % everyone
        pl.semaphore_signal(
            barrier, inc=1, device_id=(other // M, other % M), device_id_type=MESH
        )

    xown = pltpu.make_async_copy(tok_ref, x_all.at[m], one_sem.at[0])
    early = [
        pltpu.make_async_copy(cos_hbm, cos_ref, one_sem.at[1]),
        pltpu.make_async_copy(sin_hbm, sin_ref, one_sem.at[2]),
        pltpu.make_async_copy(wout_hbm, wout_ref, one_sem.at[3]),
    ]
    for b in range(S):
        early.append(pltpu.make_async_copy(
            tok_ref.at[pl.ds((b + 1) * L - 16, 16), :], tail_tok.at[b], one_sem.at[4 + b]
        ))
    pl.semaphore_wait(barrier, everyone - 1)

    pending = []

    def remote(src, dst, ss, rs, to, cond=None):
        cp = pltpu.make_async_remote_copy(
            src_ref=src, dst_ref=dst, send_sem=ss, recv_sem=rs, device_id=to, device_id_type=MESH
        )
        if cond is None:
            cp.start()
        else:
            pl.when(cond)(cp.start)
        pending.append((cp, cond))

    def local(src, dst, rs, cond=None):
        cp = pltpu.make_async_copy(src, dst, rs)
        if cond is None:
            cp.start()
        else:
            pl.when(cond)(cp.start)

    def arrive(buf, sem, n):
        for i in range(n):
            pltpu.make_async_copy(buf.at[i], buf.at[i], sem.at[i]).wait()

    def xsend(hop, c, side):
        rr = pl.ds(c * xpiece, xpiece)
        owner = m - hop if side == 0 else m + hop
        to = m + 1 if side == 0 else m - 1
        return pltpu.make_async_remote_copy(
            src_ref=(tok_ref.at[rr, :] if hop == 0 else x_all.at[owner, rr, :]),
            dst_ref=x_all.at[owner, rr, :],
            send_sem=xs_sem.at[hop, c, side],
            recv_sem=xr_sem.at[hop, c, side],
            device_id=(d, to),
            device_id_type=MESH,
        )

    def xpred(hop, side):
        if side == 0:
            return (m < M - 1) & (m - hop >= 0)
        return (m > 0) & (m + hop < M)

    def xstart(hop, c):
        for side in range(2):
            @pl.when(xpred(hop, side))
            def _(side=side):
                xsend(hop, c, side).start()

    def xwait(hop, c):
        rr = pl.ds(c * xpiece, xpiece)
        for side in range(2):
            owner = m - hop - 1 if side == 0 else m + hop + 1
            ok = (m - hop - 1 >= 0) if side == 0 else (m + hop + 1 < M)

            @pl.when(ok)
            def _(side=side, owner=owner):
                pltpu.make_async_copy(
                    x_all.at[owner, rr, :], x_all.at[owner, rr, :], xr_sem.at[hop, c, side]
                ).wait()

    def wcopy(mask, p, c, bit, send_sem, recv_sem):
        owner = flip(d, mask)
        rr = wrows(p, c)
        remote(w_all.at[owner, rr, :], w_all.at[owner, rr, :], send_sem, recv_sem,
               (flip(d, bit), m))

    def wsend(mask, p, c, step):
        bit = plan[p][0][step]
        wcopy(mask, p, c, bit, ps_sem.at[p, mask // 2, c, step],
              pr_sem.at[p, (mask ^ bit) // 2, c])

    def csend(mask, p, c):
        wcopy(mask, p, c, 1, cs_sem.at[p, mask // 2, c], cr_sem.at[p, mask // 2, c])

    def wwait(mask, p, c, sem):
        owner = flip(d, mask)
        rr = wrows(p, c)
        pltpu.make_async_copy(w_all.at[owner, rr, :], w_all.at[owner, rr, :], sem).wait()

    steps = len(plan[0][0])
    for i, (p, c, trio) in enumerate(own):
        for cp in trio:
            cp.wait()
        wsend(0, p, c, 0)
        if i == parts - 1:
            for cc in range(xchunks):
                xstart(0, cc)
    for step in range(1, steps):
        for c in range(chunks):
            for p in range(parts):
                wsend(0, p, c, step)
    for c in range(chunks):
        for p in range(parts):
            csend(0, p, c)
    xown.start()
    for cp in early:
        cp.start()
    for i in range(1, D):
        to = (d + i) % D
        remote(contrib_ref.at[to], dir_all.at[d], s2.at[i], r2.at[d], (to, m))
    local(contrib_ref.at[d], dir_all.at[d], r2.at[d])

    rounds = len(plan[0][1])
    wevents = [(r, c) for r in range(rounds) for c in range(chunks)]
    xevents = [(h, c) for h in range(M - 1) for c in range(xchunks)]
    merged = sorted(
        [((i + 1) / len(wevents), 1, e) for i, e in enumerate(wevents)]
        + [(0.8 * (i + 1) / len(xevents), 0, e) for i, e in enumerate(xevents)]
    )

    def use(owner, lo, n):
        base = owner * depth
        shard = base // width
        col = pl.multiple_of(base % width + lo, 128 if n % 128 == 0 else n)
        acc[...] += jnp.dot(
            x_all[shard, :, pl.ds(col, n)], w_all[owner, pl.ds(lo, n), :],
            preferred_element_type=F32,
        )

    every_piece = {(p, c) for p in range(parts) for c in range(chunks)}
    got = {0: set(every_piece)}
    used = set()
    late = []
    todo = []

    def sweep(left):
        whole = [k for k in got if got[k] == every_piece and not any((k, q) in used for q in every_piece)]
        for mask in whole:
            todo.append((mask, False))
            used.update((mask, q) for q in every_piece)
        todo.extend((mask, True) for mask in whole)
        fresh = sorted((k, q) for k in got for q in got[k] if (k, q) not in used)
        if piece % 128:
            fresh = []
        for mask, (p, c) in fresh:
            used.add((mask, (p, c)))
            use(flip(d, mask), (p * chunks + c) * piece, piece)
        finish()
        late.extend(fresh)
        drain(-(-len(todo) // max(1, left - 1)))

    def drain(n):
        for mask, paired in todo[:n]:
            if paired:
                for p, c in sorted(every_piece):
                    wwait(mask + 1, p, c, cr_sem.at[p, mask // 2, c])
            use(flip(d, mask + int(paired)), 0, depth)
        del todo[:n]

    def finish():
        for mask, (p, c) in late:
            wwait(mask + 1, p, c, cr_sem.at[p, mask // 2, c])
            use(flip(d, mask + 1), (p * chunks + c) * piece, piece)
        late.clear()

    x_left = len(xevents)
    for _, kind, (a, c) in merged:
        if kind == 0:
            xwait(a, c)
            if a + 1 < M - 1:
                xstart(a + 1, c)
            x_left -= 1
            if x_left == 0:
                xown.wait()
                total = jnp.zeros((rows, 1), F32)
                for k in range(M):
                    xv = x_all[k].astype(F32)
                    total = total + jnp.sum(xv * xv, axis=1, keepdims=True)
                inv = lax.rsqrt(total / model_width + 1e-05)
                for h in range(M - 1):
                    for cc in range(xchunks):
                        for side in range(2):
                            @pl.when(xpred(h, side))
                            def _(h=h, cc=cc, side=side):
                                xsend(h, cc, side).wait_send()
                for k in range(M):
                    g = gain_ref[k * width:(k + 1) * width].astype(F32).reshape(1, width)
                    x_all[k] = (x_all[k].astype(F32) * inv * g).astype(BF16)
                acc[...] = jnp.zeros_like(acc)
        else:
            for p in range(parts):
                mask, step = plan[p][1][a]
                wwait(mask, p, c, pr_sem.at[p, mask // 2, c])
                for later in range(step + 1, steps):
                    wsend(mask, p, c, later)
                csend(mask, p, c)
                got.setdefault(mask, set()).add((p, c))
            if x_left == 0:
                sweep(len(wevents) - wevents.index((a, c)))
    drain(len(todo))
    finish()

    for cp in early:
        cp.wait()
    half = HEAD_SIZE // 2

    def rope(x, cos, sin):
        turned = jnp.concatenate([x[:, half:], x[:, :half]], axis=1)
        return (x * cos + turned * sin).astype(BF16)

    def softmax(logits):
        e = jnp.exp(logits - jnp.max(logits, axis=1, keepdims=True))
        return (e * (1.0 / jnp.sum(e, axis=1, keepdims=True))).astype(BF16)

    def scaled(q, k):
        return lax.dot_general(
            q, k, (((1,), (1,)), ((), ())), preferred_element_type=F32
        ) * (1.0 / math.sqrt(HEAD_SIZE))

    for b in range(S):
        span_b = slice(b * L, (b + 1) * L)
        at_last = (b + 1) * L - 1
        for n in range(kv_heads):
            lo = qw + n * HEAD_SIZE
            k = rope(acc[span_b, lo:lo + HEAD_SIZE], cos_ref[...], sin_ref[...])
            v = acc[span_b, lo + kw:lo + kw + HEAD_SIZE].astype(BF16)
            k_s[b * kv_heads + n] = k
            v_s[b * kv_heads + n] = v
            for g in range(G):
                h = n * G + g
                q_s[g:g + 1, :] = acc[at_last:at_last + 1, h * HEAD_SIZE:(h + 1) * HEAD_SIZE]
            q = rope(q_s[...], cos_ref[L - 1:L, :], sin_ref[L - 1:L, :])
            mixed = jnp.dot(softmax(scaled(q, k)), v, preferred_element_type=F32)
            mixed = mixed.astype(BF16).astype(F32)
            for g in range(G):
                h = n * G + g
                last_src[b:b + 1, h * HEAD_SIZE:(h + 1) * HEAD_SIZE] = mixed[g:g + 1, :]
    for i in range(1, D):
        to = (d + i) % D
        remote(last_src, last_all.at[d], s1.at[i], r1.at[d], (to, m))
    local(last_src, last_all.at[d], r1.at[d])

    ahead = lax.broadcasted_iota(jnp.int32, (L, L), 0) >= lax.broadcasted_iota(jnp.int32, (L, L), 1)

    def attend(first, end):
        for b in range(S):
            @pl.loop(first, end)
            def _(h):
                at = pl.ds(pl.multiple_of(h * HEAD_SIZE, HEAD_SIZE), HEAD_SIZE)
                n = b * kv_heads + h // G
                q = rope(acc[pl.ds(b * L, L), at], cos_ref[...], sin_ref[...])
                logits = jnp.where(ahead, scaled(q, k_s[n]), -1e30)
                mixed = jnp.dot(softmax(logits), v_s[n], preferred_element_type=F32).astype(BF16)
                head_ref[pl.ds(b * L, L), at] = mixed
                column = jnp.sum(mixed.astype(F32), axis=0, keepdims=True)
                if b == 0:
                    tot_src[:, at] = column
                else:
                    tot_src[:, at] += column

    cut = heads * 3 // 8
    attend(0, cut)
    arrive(last_all, r1, D)
    for j in range(D):
        rows_a[j * S:(j + 1) * S, 0:qw] = last_all[j]
    w = wout_ref[...]
    partial = jnp.dot(rows_a[:, 0:qw].astype(BF16), w, preferred_element_type=F32)
    for j in range(D):
        out_src[j] = partial[j * S:(j + 1) * S, :]
    span = d // R
    slot = (d % R) * M + m
    for i in range(D):
        to = (d + i) % D
        if i == 0:
            remote(out_src.at[to], out_all.at[slot], s3.at[i], r3.at[slot], (to, span), m != span)
            local(out_src.at[to], out_all.at[slot], r3.at[slot], m == span)
        else:
            remote(out_src.at[to], out_all.at[slot], s3.at[i], r3.at[slot], (to, span))

    attend(cut, heads)
    for i in range(1, D):
        to = (d + i) % D
        remote(tot_src, tot_all.at[d], s4.at[i], r4.at[d], (to, m))
    local(tot_src, tot_all.at[d], r4.at[d])
    arrive(dir_all, r2, D)
    direction = dir_all[0]
    for j in range(1, D):
        direction = direction + dir_all[j]
    weighted = fgain_ref[...].astype(F32).reshape(1, width) * direction

    arrive(out_all, r3, D)
    pieces = []
    for jj in range(R):
        part_sum = out_all[jj * M]
        for k in range(1, M):
            part_sum = part_sum + out_all[jj * M + k]
        pieces.append(part_sum)
    attn_last = jnp.concatenate(pieces, axis=1).astype(BF16).astype(F32)
    toks = [tail_tok[b].astype(F32)[15:16, :] for b in range(S)]
    residual = (toks[0] if S == 1 else jnp.concatenate(toks, axis=0)) + attn_last
    sq_src[0] = jnp.broadcast_to(jnp.sum(residual * residual, axis=1, keepdims=True), (S, 128))
    sq_src[1] = jnp.broadcast_to(jnp.sum(residual * weighted, axis=1, keepdims=True), (S, 128))
    for i in range(1, M):
        to = (m + i) % M
        remote(sq_src, sq_all.at[m], s5.at[i], r5.at[m], (d, to))
    local(sq_src, sq_all.at[m], r5.at[m])
    for jj in range(R):
        g_src[jj, 0:S, :] = weighted[:, jj * cols:(jj + 1) * cols]
        g_src[jj, S:2 * S, :] = residual[:, jj * cols:(jj + 1) * cols]
    for i in range(M - 1, -1, -1):
        k = (m + i) % M
        for jj in range(R):
            to = m * R + jj
            if i == 0:
                remote(g_src.at[jj], g_all.at[d], s6.at[jj, i], r6.at[d], (to, k), to != d)
                local(g_src.at[jj], g_all.at[d], r6.at[d], to == d)
            else:
                remote(g_src.at[jj], g_all.at[d], s6.at[jj, i], r6.at[d], (to, k))
    arrive(sq_all, r5, M)
    square = sq_all[0, 0]
    product = sq_all[0, 1]
    for k in range(1, M):
        square = square + sq_all[k, 0]
        product = product + sq_all[k, 1]
    inverse = lax.rsqrt(square / model_width + 1e-05)
    metric = inverse * product
    metric_ref[...] = metric[:, 0:1]
    fall = (metric * inverse * inverse / model_width)[:, 0:1]
    arrive(tot_all, r4, D)
    mean = tot_all[0]
    for j in range(1, D):
        mean = mean + tot_all[j]
    mean = mean / token_count
    arrive(g_all, r6, D)
    for j in range(D):
        rows_g[2 * j * S:2 * (j + 1) * S, :] = g_all[j]
    exact = rows_g[...]
    coarse = exact.astype(BF16)
    fine = (exact - coarse.astype(F32)).astype(BF16)
    both = lax.dot_general(
        jnp.concatenate([coarse, fine], axis=0), w, (((1,), (1,)), ((), ())),
        preferred_element_type=F32,
    )
    hg = both[:2 * D * S] + both[2 * D * S:]
    for j in range(D):
        hg_src[j] = hg[2 * j * S:2 * (j + 1) * S, :]
    for i in range(1, D):
        to = (d + i) % D
        remote(hg_src.at[to], hg_all.at[d], s7.at[i], r7.at[d], (to, m))
    local(hg_src.at[d], hg_all.at[d], r7.at[d])
    arrive(hg_all, r7, D)
    joint = hg_all[0]
    for j in range(1, D):
        joint = joint + hg_all[j]
    grads = joint[0:S] * inverse[:, 0:1] - joint[S:2 * S] * fall
    gap = (mean - last_src[...]) * grads
    lane = lax.broadcasted_iota(jnp.int32, (S, heads), 1)
    scores = jnp.zeros((S, heads), F32)
    for h in range(heads):
        part = jnp.sum(gap[:, h * HEAD_SIZE:(h + 1) * HEAD_SIZE], axis=1, keepdims=True)
        scores = jnp.where(lane == h, part, scores)
    scores_ref[...] = scores
    for cp, cond in pending:
        if cond is None:
            cp.wait_send()
        else:
            pl.when(cond)(cp.wait_send)


def tables():
    half = HEAD_SIZE // 2
    inv_freq = np.exp(np.arange(half) * (-2.0 * math.log(500000.0) / HEAD_SIZE))
    angles = np.arange(SEQUENCE_LENGTH)[:, None] * inv_freq[None, :]
    c, s = np.cos(angles), np.sin(angles)
    cos = np.concatenate([c, c], axis=1).astype(np.float32)
    return cos, np.concatenate([-s, s], axis=1).astype(np.float32)


def whole(D, M, tokens, gain, wq, wk, wv, w_out, contrib, final_gain):
    rows, width = tokens.shape
    S = rows // SEQUENCE_LENGTH
    depth = wq.shape[0]
    entries, cols = w_out.shape
    total = wq.shape[1] + wk.shape[1] + wv.shape[1]
    heads, kv_heads = wq.shape[1] // HEAD_SIZE, wk.shape[1] // HEAD_SIZE
    parts = len(spread_plan(D))
    steps = len(spread_plan(D)[0][0])
    chunks = max(1, min(4, depth // (128 * parts)))
    xchunks = 2
    half = D // 2
    R = D // M
    cos, sin = tables()
    DMA = pltpu.SemaphoreType.DMA
    ANY = pl.BlockSpec(memory_space=pl.ANY)
    V = pl.BlockSpec(memory_space=pltpu.VMEM)

    def f(*shape):
        return pltpu.VMEM(shape, F32)

    def h(*shape):
        return pltpu.VMEM(shape, BF16)

    return pl.pallas_call(
        functools.partial(whole_kernel, D, M, chunks, xchunks, rows * D),
        name="whole",
        out_shape=[
            jax.ShapeDtypeStruct((rows, entries), BF16),
            jax.ShapeDtypeStruct((S, heads), F32),
            jax.ShapeDtypeStruct((S, 1), F32),
        ],
        in_specs=[ANY, V, ANY, ANY, ANY, ANY, ANY, ANY, ANY, V],
        out_specs=[V, V, V],
        scratch_shapes=[
            h(M, rows, width), h(D, depth, total), f(rows, total),
            f(SEQUENCE_LENGTH, HEAD_SIZE), f(SEQUENCE_LENGTH, HEAD_SIZE),
            h(entries, cols), h(S, 16, width), f(heads // kv_heads, HEAD_SIZE),
            h(S * kv_heads, SEQUENCE_LENGTH, HEAD_SIZE), h(S * kv_heads, SEQUENCE_LENGTH, HEAD_SIZE),
            f(1, entries), f(S, entries), f(D, 1, entries), f(D, S, entries),
            f(D * S, max(entries, cols)), f(D, S, cols), f(D, S, cols), f(D, S, width),
            f(2, S, 128), f(M, 2, S, 128), f(R, 2 * S, cols), f(D, 2 * S, cols),
            f(D, 2 * S, entries), f(D, 2 * S, entries), f(2 * D * S, cols),
            DMA((parts, chunks, 3)), DMA((4 + S,)),
            DMA((M - 1, xchunks, 2)), DMA((M - 1, xchunks, 2)),
            DMA((parts, half, chunks, steps)), DMA((parts, half, chunks)),
            DMA((parts, half, chunks)), DMA((parts, half, chunks)),
            DMA((D,)), DMA((D,)), DMA((D,)), DMA((D,)), DMA((D,)), DMA((D,)), DMA((D,)), DMA((D,)),
            DMA((M,)), DMA((M,)), DMA((R, M)), DMA((D,)), DMA((D,)), DMA((D,)),
        ],
        compiler_params=pltpu.CompilerParams(
            collective_id=0, has_side_effects=True, vmem_limit_bytes=56 * 1024 * 1024
        ),
    )(tokens, gain, wq, wk, wv, jnp.asarray(cos), jnp.asarray(sin), w_out, contrib,
      final_gain)


GROUP = 16


def pick_kernel(per, vocab_rows, clean_ref, corrupt_ref, *refs):
    blocks, out_ref = refs[:-1], refs[-1]
    step = pl.program_id(0)
    start = lax.axis_index("dp") * vocab_rows
    where = lax.broadcasted_iota(jnp.int32, (GROUP, 1), 0)
    for i in range(per):
        rows = []
        for side in range(2):
            at = (clean_ref, corrupt_ref)[side][step * per + i] - start
            block = blocks[side * per + i][...].astype(F32)
            hit = (where == at % GROUP) & (at >= 0) & (at < vocab_rows)
            rows.append(jnp.sum(jnp.where(hit, block, 0.0), axis=0, keepdims=True))
        out_ref[i] = rows[0] - rows[1]


def pick(unembed, clean_ids, corrupt_ids):
    vocab_rows, width = unembed.shape
    n = clean_ids.shape[0]
    per = min(8, n)

    def spec(side, i):
        def index(step, *ids):
            at = ids[side][step * per + i] - lax.axis_index("dp") * vocab_rows
            return jnp.clip(at, 0, vocab_rows - 1) // GROUP, 0
        return pl.BlockSpec((GROUP, width), index)

    return pl.pallas_call(
        functools.partial(pick_kernel, per, vocab_rows),
        name="pick",
        grid_spec=pltpu.PrefetchScalarGridSpec(
            num_scalar_prefetch=2,
            grid=(n // per,),
            in_specs=[spec(side, i) for side in range(2) for i in range(per)],
            out_specs=pl.BlockSpec((per, 1, width), lambda step, *ids: (step, 0, 0)),
        ),
        out_shape=jax.ShapeDtypeStruct((n, 1, width), F32),
    )(clean_ids, corrupt_ids, *([unembed] * (2 * per)))


def per_device(
    D, M, tokens, attn_gain, w_query, key_w, value_w, w_out, final_gain, unembed,
    clean_ids, corrupt_ids,
):
    S = tokens.shape[0] // SEQUENCE_LENGTH
    width = unembed.shape[1]
    contrib = pick(unembed, clean_ids, corrupt_ids).reshape(D, S, width)
    head_out, scores, metric = whole(
        D, M, tokens, attn_gain, w_query, key_w, value_w, w_out, contrib, final_gain
    )
    return head_out, scores, metric.reshape(S)


def solution(mesh):
    in_specs = (
        P("dp", "mp"), P(), P("dp", "mp"), P("dp", "mp"), P("dp", "mp"),
        P("mp", "dp"), P("mp"), P("dp", "mp"), P(), P(),
    )
    out_specs = (P("dp", "mp"), P("dp", "mp"), P("dp"))
    return jax.shard_map(
        functools.partial(per_device, mesh.shape["dp"], mesh.shape["mp"]),
        mesh=mesh, in_specs=in_specs, out_specs=out_specs, check_vma=False,
    )
```
